32 devices in a mesh: grp: 2 (over y), tm: 8 (over z, x), space: 2 (over core).
Axes of the slice: x: 2, y: 2, z: 4, core: 2. Of those that a mesh axis runs over, the one named last changes fastest.
Arguments:
- tokens: bfloat16 [16, 24, 64, 1024], P(('grp', 'tm'), 'space'), parts along dimension 0, may hold values from -28 to 28
- gains: float32 [2, 1024], replicated, may hold values from 0.5 to 2
- qkv_weights: bfloat16 [2, 1024, 1536], replicated, may hold values from -1.125 to 1.125
- out_weights: bfloat16 [2, 512, 1024], replicated, may hold values from -0.25 to 0.25
Outputs:
- video_out: bfloat16 [16, 24, 64, 1024], P(('grp', 'tm'), 'space'), parts along dimension 0
The draws below stay inside these ranges and needn't reach their ends.
There are 2 independent parts, one for each index of `grp`. The reference program is written for one: setup_inputs(seed, part) draws one part's arguments, and reference() takes and returns one part's arrays. A program takes and returns all parts, laid end to end along the dimension named above; an argument that names none is the same for every part. Nothing has to cross between parts.
All inputs are finite; a program needn't handle non-finite values.
Results may differ from the reference program's by a relative error of at most 0.007.
Values may be sent and summed in bfloat16 or wider, within the bound.
No kernel may reach another device: no remote copies, remote signals or barrier semaphores. Data moves between devices by JAX's collectives and lax.ppermute only.
A program may use at most 64 MiB of HBM per device.

```python
import math
import jax
import jax.numpy as jnp
from jax import lax

D = 1024
HEADS = 8
HEAD = 64
COLS = 64
HEIGHT = 24
FRAMES = 8


def draw_tokens(key, part):
    full_shape = (FRAMES, HEIGHT, COLS, D)
    return jnp.clip(jax.random.normal(key, full_shape, jnp.float32), -6.0, 6.0).astype(jnp.bfloat16)


def draw_qkv_weights(key, part):
    inner_width = HEADS * HEAD
    full_shape = (2, D, 3 * inner_width)
    key_main = jax.random.fold_in(key, 0)
    matrix = jnp.clip(jax.random.normal(key_main, full_shape, jnp.float32), -6.0, 6.0) / math.sqrt(D)
    return matrix.astype(jnp.bfloat16)


def gaussian(key, shape, width, bound, held_as=jnp.bfloat16):
    entries = jax.random.normal(key, shape, jnp.float32) * width
    return jnp.minimum(jnp.maximum(entries, -bound), bound).astype(held_as)


def setup_inputs(seed: int = 0, part: int = 0) -> dict:
    splits = jax.random.split(jax.random.key(seed), 5)
    part_splits = jax.random.split(jax.random.fold_in(splits[4], part), 5)
    return {
        "tokens": draw_tokens(jax.random.fold_in(jax.random.fold_in(splits[4], part), 71), part),
        "gains": jnp.clip(jnp.exp(jax.random.uniform(splits[1], (2, D), jnp.float32, math.log(0.5), math.log(2.0))), 0.5, 2.0),
        "qkv_weights": draw_qkv_weights(jax.random.fold_in(splits[4], 71), part),
        "out_weights": gaussian(splits[3], (2, HEADS * HEAD, D), (HEADS * HEAD) ** -0.5, 0.25),
    }


def attend_groups(stream, gain_row, qkv_weight, out_weight):
    group_n, length, feat_count = stream.shape
    widened = stream.astype(jnp.float32)
    normed = (widened * lax.rsqrt(lax.optimization_barrier(jnp.mean(widened * widened, axis=-1, keepdims=True)) + 1e-06) * gain_row).astype(jnp.bfloat16)
    projected = jnp.dot(normed.reshape(group_n * length, feat_count), qkv_weight, preferred_element_type=jnp.float32).astype(jnp.bfloat16)
    shaped = projected.reshape(group_n, length, 3, HEADS, HEAD).astype(jnp.float32)
    scores = jnp.einsum('gqhd,gkhd->ghqk', shaped[:, :, 0], shaped[:, :, 1]) * HEAD ** (-0.5)
    row_max = lax.optimization_barrier(jnp.max(scores, axis=-1, keepdims=True))
    raised = jnp.exp(scores - row_max)
    weights = (raised / lax.optimization_barrier(jnp.sum(raised, axis=-1, keepdims=True))).astype(jnp.bfloat16)
    mixture = jnp.einsum('ghqk,gkhd->gqhd', weights.astype(jnp.float32), shaped[:, :, 2]).astype(jnp.bfloat16)
    mixture = mixture.reshape(group_n * length, HEADS * HEAD)
    update = jnp.dot(mixture, out_weight, preferred_element_type=jnp.float32).reshape(group_n, length, feat_count)
    return (widened + update).astype(jnp.bfloat16)

def reference(tokens, gains, qkv_weights, out_weights):
    frame_n, height_n, column_n, feat_count = tokens.shape
    by_column = jnp.transpose(tokens, (0, 2, 1, 3)).reshape(frame_n * column_n, height_n, feat_count)
    spatial = attend_groups(by_column, gains[0], qkv_weights[0], out_weights[0]).reshape(frame_n, column_n, height_n, feat_count)
    by_frame = jnp.transpose(spatial, (2, 1, 0, 3)).reshape(height_n * column_n, frame_n, feat_count)
    temporal = attend_groups(by_frame, gains[1], qkv_weights[1], out_weights[1]).reshape(height_n, column_n, frame_n, feat_count)
    return jnp.transpose(temporal, (2, 0, 1, 3))
```

```python
import functools

import jax
import jax.numpy as jnp
from jax import lax
from jax.experimental import pallas as pl
from jax.experimental.pallas import tpu as pltpu
from jax.sharding import PartitionSpec as P

HEAD = 64
EPS = 1e-06
QUAD = 4
CHUNKS = 2
COLB = 8
POSB = 16
NEG = -1e30


def params():
    return pltpu.CompilerParams(vmem_limit_bytes=40 * 1024 * 1024)


def normalise(stream, gain):
    scale = lax.rsqrt(jnp.mean(stream * stream, axis=-1, keepdims=True) + EPS)
    return (stream * scale * gain).astype(jnp.bfloat16)


def head_lanes(rows, width):
    return lax.broadcasted_iota(jnp.int32, (rows, width), 1) // HEAD


def same_group(queries, keys, group):
    left = lax.broadcasted_iota(jnp.int32, (queries, keys), 0) % group
    right = lax.broadcasted_iota(jnp.int32, (queries, keys), 1) % group
    return left == right


def attend_quad(query, key, value, keep):
    rows, width = query.shape
    lanes = head_lanes(rows, width)
    heads = width // HEAD
    zero = jnp.zeros_like(query)
    stacked = jnp.concatenate([jnp.where(lanes == h, query, zero) for h in range(heads)], axis=0)
    scores = lax.dot_general(
        stacked, key, (((1,), (1,)), ((), ())), preferred_element_type=jnp.float32
    )
    scores = jnp.where(keep, scores, NEG)
    raised = jnp.exp(scores - jnp.max(scores, axis=-1, keepdims=True))
    total = jnp.sum(raised, axis=-1, keepdims=True)
    mixed = jnp.dot(raised.astype(jnp.bfloat16), value, preferred_element_type=jnp.float32)
    mixed = mixed * (1.0 / total)
    out = mixed[:rows]
    for h in range(1, heads):
        out = jnp.where(lanes == h, mixed[h * rows : (h + 1) * rows], out)
    return out.astype(jnp.bfloat16)


def project_kernel(x_ref, gain_ref, w_ref, q_ref, kv_ref):
    rows, cols, feat = x_ref.shape
    inner = q_ref.shape[1]
    per = rows * COLB
    parts = [
        normalise(
            x_ref[:, b * COLB : (b + 1) * COLB, :].astype(jnp.float32).reshape(per, feat),
            gain_ref[...],
        )
        for b in range(cols // COLB)
    ]
    normed = jnp.concatenate(parts, axis=0)
    kv_ref[...] = jnp.dot(
        normed, w_ref[:, inner:], preferred_element_type=jnp.float32
    ).astype(jnp.bfloat16)
    q_ref[...] = jnp.dot(
        normed, w_ref[:, :inner], preferred_element_type=jnp.float32
    ).astype(jnp.bfloat16) * jnp.bfloat16(HEAD**-0.5)


def height_kernel(me_ref, x_ref, q_ref, kv_ref, other_ref, w_ref, *refs):
    full_ref, mix_ref = refs[-2], refs[-1]
    piece_refs = refs[:-2]
    rows, cols, feat = x_ref.shape
    inner = q_ref.shape[1]
    per = rows * COLB
    width = QUAD * HEAD
    keep = same_group(QUAD * per, 2 * per, COLB)

    def block(b, carry):
        span = pl.ds(pl.multiple_of(b * per, per), per)
        for g in range(inner // width):
            lo = slice(g * width, (g + 1) * width)
            hi = slice(inner + g * width, inner + (g + 1) * width)
            key = jnp.concatenate([kv_ref[span, lo], other_ref[span, lo]], axis=0)
            value = jnp.concatenate([kv_ref[span, hi], other_ref[span, hi]], axis=0)
            mix_ref[span, lo] = attend_quad(q_ref[span, lo], key, value, keep)
        return carry

    lax.fori_loop(0, cols // COLB, block, 0)
    for b in range(cols // COLB):
        stream = x_ref[:, b * COLB : (b + 1) * COLB, :].astype(jnp.float32).reshape(per, feat)
        update = jnp.dot(
            mix_ref[b * per : (b + 1) * per, :], w_ref[...], preferred_element_type=jnp.float32
        )
        full_ref[b * per : (b + 1) * per, :] = (stream + update).astype(jnp.bfloat16)
    me = me_ref[0]
    each = piece_refs[0].shape[0]
    for k, piece_ref in enumerate(piece_refs):
        start = pl.multiple_of(jnp.bitwise_xor(me, k) * each, each)
        piece_ref[...] = full_ref[pl.ds(start, each), :]


def time_kernel(*refs):
    frames = (len(refs) - 3) // 2
    in_refs = refs[:frames]
    gain_ref, w_ref = refs[frames : frames + 2]
    out_refs = refs[frames + 2 : 2 * frames + 2]
    qkv_ref = refs[-1]
    each, feat = in_refs[0].shape
    inner = out_refs[0].shape[1]
    normed = jnp.concatenate(
        [normalise(ref[...].astype(jnp.float32), gain_ref[...]) for ref in in_refs], axis=0
    )
    qkv_ref[...] = jnp.dot(normed, w_ref[...], preferred_element_type=jnp.float32).astype(
        jnp.bfloat16
    )
    width = QUAD * HEAD
    keep = same_group(QUAD * frames * POSB, frames * POSB, POSB)

    def gather(start, lo):
        return jnp.concatenate(
            [qkv_ref[k * each + start : k * each + start + POSB, lo : lo + width] for k in range(frames)],
            axis=0,
        )

    for p in range(each // POSB):
        for g in range(inner // width):
            lo = g * width
            query = gather(p * POSB, lo) * jnp.bfloat16(HEAD**-0.5)
            out = attend_quad(
                query, gather(p * POSB, inner + lo), gather(p * POSB, 2 * inner + lo), keep
            )
            for k in range(frames):
                out_refs[k][p * POSB : (p + 1) * POSB, lo : lo + width] = out[
                    k * POSB : (k + 1) * POSB
                ]


def finish_kernel(me_ref, full_ref, w_ref, *refs):
    out_ref, mix_ref = refs[-2:]
    in_refs = refs[:-2]
    rows, cols, feat = out_ref.shape
    per = rows * COLB
    me = me_ref[0]
    each = in_refs[0].shape[0]
    for k, ref in enumerate(in_refs):
        start = pl.multiple_of(jnp.bitwise_xor(me, k) * each, each)
        mix_ref[pl.ds(start, each), :] = ref[...]
    for b in range(cols // COLB):
        update = jnp.dot(
            mix_ref[b * per : (b + 1) * per, :], w_ref[...], preferred_element_type=jnp.float32
        )
        total = full_ref[b * per : (b + 1) * per, :].astype(jnp.float32) + update
        out_ref[:, b * COLB : (b + 1) * COLB, :] = total.reshape(rows, COLB, feat).astype(
            jnp.bfloat16
        )


VMEM = pl.BlockSpec(memory_space=pltpu.VMEM)
SMEM = pl.BlockSpec(memory_space=pltpu.SMEM)


def cost(flops, moved):
    return pl.CostEstimate(flops=int(flops), bytes_accessed=int(moved), transcendentals=0)


def fast(tokens, gains, qkv_weights, out_weights):
    frames = lax.axis_size("tm")
    me = lax.axis_index("tm").astype(jnp.int32)[None]
    rows, cols, feat = tokens.shape[1:]
    inner = out_weights.shape[1]
    wide = cols // CHUNKS
    count = rows * wide
    each = count // frames
    bf = jnp.bfloat16

    def pick(i, n):
        return pl.BlockSpec((None,) + n, lambda _: (i,) + (0,) * len(n))

    def columns(c):
        return pl.BlockSpec((rows, wide, feat), lambda _: (0, c, 0))

    def whole(*shape):
        return pl.BlockSpec(shape, lambda _: (0,) * len(shape))

    x = tokens[0]
    gain3 = gains[:, None, :]

    def project(c):
        return pl.pallas_call(
            project_kernel,
            grid=(1,),
            in_specs=[columns(c), pick(0, (1, feat)), pick(0, (feat, 3 * inner))],
            out_specs=[whole(count, inner), whole(count, 2 * inner)],
            out_shape=[
                jax.ShapeDtypeStruct((count, inner), bf),
                jax.ShapeDtypeStruct((count, 2 * inner), bf),
            ],
            compiler_params=params(),
            cost_estimate=cost(6 * count * feat * inner, 2 * feat * 3 * inner + 5 * count * feat),
            name="project",
        )(x, gain3, qkv_weights)

    def height(c, q, kv, other):
        outs = pl.pallas_call(
            height_kernel,
            grid=(1,),
            in_specs=[
                SMEM,
                columns(c),
                whole(count, inner),
                whole(count, 2 * inner),
                whole(count, 2 * inner),
                pick(0, (inner, feat)),
            ],
            out_specs=[whole(each, feat)] * frames + [whole(count, feat)],
            out_shape=[jax.ShapeDtypeStruct((each, feat), bf)] * frames
            + [jax.ShapeDtypeStruct((count, feat), bf)],
            scratch_shapes=[pltpu.VMEM((count, inner), bf)],
            compiler_params=params(),
            cost_estimate=cost(6 * count * feat * inner, 2 * feat * inner + 12 * count * feat),
            name="height",
        )(me, x, q, kv, other, out_weights)
        return outs[:-1], outs[-1]

    def timed(pieces):
        return pl.pallas_call(
            time_kernel,
            grid=(1,),
            in_specs=[whole(each, feat)] * frames
            + [pick(1, (1, feat)), pick(1, (feat, 3 * inner))],
            out_specs=[whole(each, inner)] * frames,
            out_shape=[jax.ShapeDtypeStruct((each, inner), bf)] * frames,
            scratch_shapes=[pltpu.VMEM((count, 3 * inner), bf)],
            compiler_params=params(),
            cost_estimate=cost(8 * count * feat * inner, 2 * feat * 3 * inner + 3 * count * feat),
            name="timed",
        )(*pieces, gain3, qkv_weights)

    def finish(c, full, mixes, prior):
        aliases = {}
        extra_specs, extra = [], []
        kernel = finish_kernel
        if prior is not None:
            aliases = {frames + 3: 0}
            extra_specs, extra = [pl.BlockSpec(memory_space=pl.ANY)], [prior]
            kernel = lambda *refs: finish_kernel(*refs[: frames + 3], *refs[frames + 4 :])
        return pl.pallas_call(
            kernel,
            grid=(1,),
            in_specs=[SMEM, whole(count, feat), pick(1, (inner, feat))]
            + [whole(each, inner)] * frames
            + extra_specs,
            out_specs=columns(c),
            out_shape=jax.ShapeDtypeStruct((rows, cols, feat), bf),
            scratch_shapes=[pltpu.VMEM((count, inner), bf)],
            input_output_aliases=aliases,
            compiler_params=params(),
            cost_estimate=cost(2 * count * feat * inner, 2 * feat * inner + 5 * count * feat),
            name="finish",
        )(me, full, out_weights, *mixes, *extra)

    pair = lax.axis_size("space")

    def swap(a):
        return lax.ppermute(a, "space", [(i, 1 - i) for i in range(pair)])

    order = sorted(range(1, frames), key=lambda k: -k)

    def exchange(pieces):
        got = [pieces[0]] + [None] * (frames - 1)
        for k in order:
            got[k] = lax.ppermute(pieces[k], "tm", [(i, i ^ k) for i in range(frames)])
        return got

    projected = [project(c) for c in range(CHUNKS)]
    others = [swap(kv) for _, kv in projected]
    heights = [height(c, *projected[c], others[c]) for c in range(CHUNKS)]
    arrived = [exchange(pieces) for pieces, _ in heights]
    mixes = [timed(pieces) for pieces in arrived]
    home = [exchange(m) for m in mixes]
    out = None
    for c in range(CHUNKS):
        out = finish(c, heights[c][1], home[c], out)
    return out[None]


def attend_plain(stream, gain, qkv_weight, out_weight):
    groups, length, feat = stream.shape
    inner = out_weight.shape[0]
    heads = inner // HEAD
    wide = stream.astype(jnp.float32)
    normed = normalise(wide, gain)
    projected = jnp.einsum(
        "glf,fe->gle", normed, qkv_weight, preferred_element_type=jnp.float32
    ).astype(jnp.bfloat16)
    q, k, v = jnp.split(projected.reshape(groups, length, 3 * heads, HEAD), 3, axis=2)
    scores = jnp.einsum("gqhd,gkhd->ghqk", q, k, preferred_element_type=jnp.float32) * HEAD**-0.5
    weights = jax.nn.softmax(scores, axis=-1).astype(jnp.bfloat16)
    mixture = jnp.einsum("ghqk,gkhd->gqhd", weights, v, preferred_element_type=jnp.float32)
    mixture = mixture.astype(jnp.bfloat16).reshape(groups, length, inner)
    update = jnp.einsum("gle,ef->glf", mixture, out_weight, preferred_element_type=jnp.float32)
    return (wide + update).astype(jnp.bfloat16)


def plain(tokens, gains, qkv_weights, out_weights):
    frames = lax.axis_size("tm")
    local = lax.all_to_all(tokens[0], "space", split_axis=1, concat_axis=0, tiled=True)
    height_n, wide, feat = local.shape
    by_column = jnp.transpose(local, (1, 0, 2))
    done = attend_plain(by_column, gains[0], qkv_weights[0], out_weights[0])
    flat = done.reshape(frames, wide * height_n // frames, feat)
    by_frame = lax.all_to_all(flat, "tm", split_axis=0, concat_axis=0, tiled=True)
    done = attend_plain(
        jnp.transpose(by_frame, (1, 0, 2)), gains[1], qkv_weights[1], out_weights[1]
    )
    back = lax.all_to_all(
        jnp.transpose(done, (1, 0, 2)), "tm", split_axis=0, concat_axis=0, tiled=True
    )
    by_row = jnp.transpose(back.reshape(wide, height_n, feat), (1, 0, 2))
    return lax.all_to_all(by_row, "space", split_axis=0, concat_axis=1, tiled=True)[None]


def solution(mesh):
    frames, pair = mesh.shape["tm"], mesh.shape["space"]

    def shards(tokens, gains, qkv_weights, out_weights):
        _, rows, cols, feat = tokens.shape
        inner = out_weights.shape[1]
        count = rows * cols // CHUNKS
        fits = (
            pair == 2
            and frames & (frames - 1) == 0
            and cols % (CHUNKS * COLB) == 0
            and count % (frames * POSB) == 0
            and inner % (QUAD * HEAD) == 0
            and feat % 128 == 0
        )
        body = fast if fits else plain
        return body(tokens, gains, qkv_weights, out_weights)

    return jax.shard_map(
        shards,
        mesh=mesh,
        in_specs=(P(("grp", "tm"), "space", None, None), P(), P(), P()),
        out_specs=P(("grp", "tm"), "space", None, None),
        check_vma=False,
    )
```

```python
import functools

import jax
import jax.numpy as jnp
from jax import lax
from jax.experimental import pallas as pl
from jax.experimental.pallas import tpu as pltpu
from jax.sharding import PartitionSpec as P


HEAD = 64
EPS = 1e-06
QUAD = 4
CHUNKS = 2
COLB = 8
POSB = 16
NEG = -1e30
VMEM_BYTES = 16 * 1024 * 1024


def params():
    return pltpu.CompilerParams(vmem_limit_bytes=VMEM_BYTES)


def normalise(stream, gain):
    scale = lax.rsqrt(jnp.mean(stream * stream, axis=-1, keepdims=True) + EPS)
    return (stream * scale * gain).astype(jnp.bfloat16)


def group_bias(keys, group):
    left = lax.broadcasted_iota(jnp.int32, (1, group, keys), 1)
    right = lax.broadcasted_iota(jnp.int32, (1, group, keys), 2) % group
    return jnp.where(left == right, 0.0, NEG)


def attend_quad(query, key, value, bias):
    rows, width = query.shape
    keys = key.shape[0]
    lanes = lax.broadcasted_iota(jnp.int32, (rows, width), 1) // HEAD
    heads = width // HEAD
    zero = jnp.zeros_like(query)
    stacked = jnp.concatenate([jnp.where(lanes == h, query, zero) for h in range(heads)], axis=0)
    scores = lax.dot_general(
        stacked, key, (((1,), (1,)), ((), ())), preferred_element_type=jnp.float32
    )
    scores = scores.reshape(heads * rows // bias.shape[1], bias.shape[1], keys) + bias
    raised = jnp.exp(scores - jnp.max(scores, axis=-1, keepdims=True))
    total = jnp.sum(raised, axis=-1, keepdims=True).reshape(heads * rows, 1)
    raised = raised.reshape(heads * rows, keys).astype(jnp.bfloat16)
    mixed = jnp.dot(raised, value, preferred_element_type=jnp.float32) * (1.0 / total)
    out = mixed[:rows]
    for h in range(1, heads):
        out = jnp.where(lanes == h, mixed[h * rows : (h + 1) * rows], out)
    return out.astype(jnp.bfloat16)


def attend(q_ref, kv_ref, other_ref, spans, group, put):
    inner = q_ref.shape[1]
    width = QUAD * HEAD
    keys = 2 * sum(size for _, size in spans[0])
    bias = group_bias(keys, group)

    def rows(ref, span, lo):
        return [ref[at : at + size, lo : lo + width] for at, size in span]

    def join(parts):
        return parts[0] if len(parts) == 1 else jnp.concatenate(parts, axis=0)

    for span in spans:
        for lo in range(0, inner, width):
            key = join(rows(kv_ref, span, lo) + rows(other_ref, span, lo))
            value = join(rows(kv_ref, span, inner + lo) + rows(other_ref, span, inner + lo))
            put(span, lo, attend_quad(join(rows(q_ref, span, lo)), key, value, bias))


def project(normed, weight, q_ref, kv_ref, inner):
    for i, lo in enumerate((inner, 2 * inner, 0)):
        part = jnp.dot(normed, weight(i), preferred_element_type=jnp.float32).astype(jnp.bfloat16)
        if lo:
            kv_ref[:, lo - inner : lo] = part
        else:
            q_ref[...] = part * jnp.bfloat16(HEAD**-0.5)


def height_project_kernel(
    c, x_ref, gain_ref, w_ref, q_ref, kv_ref, x_buf, w_buf, gain_buf, x_sem, w_sem, gain_sem
):
    blocks, rows, colb, feat = x_buf.shape
    inner = q_ref.shape[1]
    loads = [
        pltpu.make_async_copy(
            x_ref.at[:, pl.ds((c * blocks + b) * colb, colb), :], x_buf.at[b], x_sem.at[b]
        )
        for b in range(blocks)
    ]
    fetches = [
        pltpu.make_async_copy(
            w_ref.at[0, :, pl.ds(lo, inner)], w_buf.at[i], w_sem.at[i]
        )
        for i, lo in enumerate((inner, 2 * inner, 0))
    ]
    gain_load = pltpu.make_async_copy(gain_ref, gain_buf, gain_sem)
    for copy in [gain_load] + loads + fetches:
        copy.start()
    gain_load.wait()
    parts = []
    for b in range(blocks):
        loads[b].wait()
        stream = x_buf[b].astype(jnp.float32).reshape(rows * colb, feat)
        parts.append(normalise(stream, gain_buf[0:1, :]))
    normed = jnp.concatenate(parts, axis=0)

    def weight(i):
        fetches[i].wait()
        return w_buf[i]

    project(normed, weight, q_ref, kv_ref, inner)


def height_kernel(
    c, hi_ref, x_ref, q_ref, kv_ref, other_ref, w_ref, *refs
):
    full_ref, mix_ref, x_buf, w_buf, x_sem, w_sem = refs[-6:]
    piece_refs = refs[:-6]
    blocks, rows, colb, feat = x_buf.shape
    per = rows * colb
    loads = [
        pltpu.make_async_copy(
            x_ref.at[:, pl.ds((c * blocks + b) * colb, colb), :], x_buf.at[b], x_sem.at[b]
        )
        for b in range(blocks)
    ]
    fetch = pltpu.make_async_copy(w_ref.at[0], w_buf, w_sem)
    fetch.start()
    for copy in loads:
        copy.start()

    def put(span, lo, out):
        at, size = span[0]
        mix_ref[at : at + size, lo : lo + out.shape[1]] = out

    attend(q_ref, kv_ref, other_ref, [[(b * per, per)] for b in range(blocks)], colb, put)
    fetch.wait()
    for b in range(blocks):
        loads[b].wait()
        stream = x_buf[b].astype(jnp.float32).reshape(per, feat)
        update = jnp.dot(
            mix_ref[b * per : (b + 1) * per, :], w_buf[...], preferred_element_type=jnp.float32
        )
        full_ref[b * per : (b + 1) * per, :] = (stream + update).astype(jnp.bfloat16)
    each = piece_refs[0].shape[0]
    for k, piece_ref in enumerate(piece_refs):
        start = pl.multiple_of(jnp.bitwise_xor(hi_ref[0], k) * each, each)
        piece_ref[...] = full_ref[pl.ds(start, each), :]


def time_project_kernel(*refs):
    gain_ref, w_ref, q_ref, kv_ref = refs[-4:]
    inner = q_ref.shape[1]
    normed = jnp.concatenate(
        [normalise(ref[...].astype(jnp.float32), gain_ref[1:2, :]) for ref in refs[:-4]], axis=0
    )
    starts = (inner, 2 * inner, 0)
    project(normed, lambda i: w_ref[:, starts[i] : starts[i] + inner], q_ref, kv_ref, inner)


def time_kernel(q_ref, kv_ref, other_ref, *mix_refs):
    each = mix_refs[0].shape[0]
    spans = [
        [(k * each + p, POSB) for k in range(len(mix_refs))] for p in range(0, each, POSB)
    ]

    def put(span, lo, out):
        at = span[0][0]
        for k, ref in enumerate(mix_refs):
            ref[at : at + POSB, lo : lo + out.shape[1]] = out[k * POSB : (k + 1) * POSB]

    attend(q_ref, kv_ref, other_ref, spans, POSB, put)


def finish_kernel(frames, hi_ref, full_ref, w_ref, *refs):
    out_ref, mix_ref = refs[-2:]
    rows, cols, feat = out_ref.shape
    per = rows * COLB
    each = refs[0].shape[0]
    for k in range(frames):
        start = pl.multiple_of(jnp.bitwise_xor(hi_ref[0], k) * each, each)
        mix_ref[pl.ds(start, each), :] = refs[k][...]
    for b in range(cols // COLB):
        update = jnp.dot(
            mix_ref[b * per : (b + 1) * per, :], w_ref[...], preferred_element_type=jnp.float32
        )
        total = full_ref[b * per : (b + 1) * per, :].astype(jnp.float32) + update
        out_ref[:, b * COLB : (b + 1) * COLB, :] = total.reshape(rows, COLB, feat).astype(
            jnp.bfloat16
        )


SMEM = pl.BlockSpec(memory_space=pltpu.SMEM)
HBM = pl.BlockSpec(memory_space=pltpu.HBM)


def cost(flops, moved):
    return pl.CostEstimate(flops=int(flops), bytes_accessed=int(moved), transcendentals=0)


def fast(tokens, gains, qkv_weights, out_weights):
    high = lax.axis_size("tm") // 2
    half = high // 2
    hi = (lax.axis_index("tm") // 2).astype(jnp.int32)[None]
    rows, cols, feat = tokens.shape[1:]
    inner = out_weights.shape[1]
    wide = cols // CHUNKS
    blocks = wide // COLB
    count = rows * wide
    each = count // high
    bf = jnp.bfloat16
    x = pltpu.with_memory_space_constraint(tokens[0], pltpu.HBM)
    gains_far = pltpu.with_memory_space_constraint(gains, pltpu.HBM)
    qkv_far = pltpu.with_memory_space_constraint(qkv_weights, pltpu.HBM)
    out_far = pltpu.with_memory_space_constraint(out_weights, pltpu.HBM)

    def pick(i, n):
        return pl.BlockSpec((None,) + n, lambda _: (i,) + (0,) * len(n))

    def whole(*shape):
        return pl.BlockSpec(shape, lambda _: (0,) * len(shape))

    def call(kernel, flops, **rest):
        return pl.pallas_call(
            kernel,
            grid=(1,),
            compiler_params=params(),
            cost_estimate=cost(flops, 4 * count * feat),
            **rest,
        )

    qkv_out = dict(
        out_specs=[whole(count, inner), whole(count, 2 * inner)],
        out_shape=[
            jax.ShapeDtypeStruct((count, inner), bf),
            jax.ShapeDtypeStruct((count, 2 * inner), bf),
        ],
    )
    qkv_in = [whole(count, inner), whole(count, 2 * inner), whole(count, 2 * inner)]
    x_scratch = pltpu.VMEM((blocks, rows, COLB, feat), bf)
    work = 2 * count * feat * inner

    def after(values, earlier):
        return lax.optimization_barrier((values, earlier))[0]

    def height_project(c, x):
        return call(
            functools.partial(height_project_kernel, c),
            3 * work,
            in_specs=[HBM, HBM, HBM],
            scratch_shapes=[
                x_scratch,
                pltpu.VMEM((3, feat, inner), bf),
                pltpu.VMEM(gains.shape, gains.dtype),
                pltpu.SemaphoreType.DMA((blocks,)),
                pltpu.SemaphoreType.DMA((3,)),
                pltpu.SemaphoreType.DMA,
            ],
            **qkv_out,
        )(x, gains_far, qkv_far)

    def height(c, q, kv, other):
        outs = call(
            functools.partial(height_kernel, c),
            4 * work,
            in_specs=[SMEM, HBM] + qkv_in + [HBM],
            out_specs=[whole(each, feat)] * high + [whole(count, feat)],
            out_shape=[jax.ShapeDtypeStruct((each, feat), bf)] * high
            + [jax.ShapeDtypeStruct((count, feat), bf)],
            scratch_shapes=[
                pltpu.VMEM((count, inner), bf),
                x_scratch,
                pltpu.VMEM((inner, feat), bf),
                pltpu.SemaphoreType.DMA((blocks,)),
                pltpu.SemaphoreType.DMA,
            ],
        )(hi, x, q, kv, other, out_far)
        return outs[:-1], outs[-1]

    def time_project(pieces):
        return call(
            time_project_kernel,
            3 * work,
            in_specs=[whole(each, feat)] * high
            + [whole(*gains.shape), pick(1, (feat, 3 * inner))],
            **qkv_out,
        )(*pieces, gains, qkv_weights)

    def timed(q, kv, other):
        return call(
            time_kernel,
            2 * work,
            in_specs=qkv_in,
            out_specs=[whole(each, inner)] * high,
            out_shape=[jax.ShapeDtypeStruct((each, inner), bf)] * high,
        )(q, kv, other)

    def finish(c, full, mixes, prior):
        aliases, extra_specs, extra = {}, [], []
        if prior is not None:
            aliases = {high + 3: 0}
            extra_specs, extra = [pl.BlockSpec(memory_space=pl.ANY)], [prior]
        return call(
            functools.partial(finish_kernel, high),
            work,
            in_specs=[SMEM, whole(count, feat), pick(1, (inner, feat))]
            + [whole(each, inner)] * high
            + extra_specs,
            out_specs=pl.BlockSpec((rows, wide, feat), lambda _: (0, c, 0)),
            out_shape=jax.ShapeDtypeStruct((rows, cols, feat), bf),
            scratch_shapes=[pltpu.VMEM((count, inner), bf)],
            input_output_aliases=aliases,
        )(hi, full, out_weights, *mixes, *extra)

    def swap(a):
        return lax.ppermute(a, "space", [(0, 1), (1, 0)])

    def route(k):
        pairs = []
        for z in range(high):
            for lo in range(2):
                for s in range(2):
                    there = z ^ k
                    to = (there * 2 + (s ^ (there >= half))) * 2 + (lo ^ (z >= half))
                    pairs.append(((z * 2 + lo) * 2 + s, to))
        return pairs

    def exchange(pieces):
        return [lax.ppermute(p, ("tm", "space"), route(k)) for k, p in enumerate(pieces)]

    def after(values, earlier):
        return lax.optimization_barrier((values, earlier))[0]

    projected, others, heights, arrived, home = [], [], [], [], []
    last = hi
    for c in range(CHUNKS):
        q, kv = height_project(c, after(x, last))
        projected.append((q, kv))
        others.append(swap(kv))
        last = q
    for c in range(CHUNKS):
        q, kv = projected[c]
        heights.append(height(c, after(q, last), kv, others[c]))
        last = heights[-1][1]
        arrived.append(exchange(heights[-1][0]))
    for c in range(CHUNKS):
        q, kv = time_project(after(arrived[c], last))
        mixes = timed(q, kv, swap(kv))
        last = mixes[0]
        home.append(exchange(mixes))
    out = None
    for c in range(CHUNKS):
        out = finish(c, after(heights[c][1], last), home[c], out)
    return out[None]


def attend_plain(stream, gain, qkv_weight, out_weight):
    groups, length, _ = stream.shape
    inner = out_weight.shape[0]
    heads = inner // HEAD
    wide = stream.astype(jnp.float32)
    normed = normalise(wide, gain)
    projected = jnp.einsum(
        "glf,fe->gle", normed, qkv_weight, preferred_element_type=jnp.float32
    ).astype(jnp.bfloat16)
    q, k, v = jnp.split(projected.reshape(groups, length, 3 * heads, HEAD), 3, axis=2)
    scores = jnp.einsum("gqhd,gkhd->ghqk", q, k, preferred_element_type=jnp.float32) * HEAD**-0.5
    weights = jax.nn.softmax(scores, axis=-1).astype(jnp.bfloat16)
    mixture = jnp.einsum("ghqk,gkhd->gqhd", weights, v, preferred_element_type=jnp.float32)
    mixture = mixture.astype(jnp.bfloat16).reshape(groups, length, inner)
    update = jnp.einsum("gle,ef->glf", mixture, out_weight, preferred_element_type=jnp.float32)
    return (wide + update).astype(jnp.bfloat16)


def plain(tokens, gains, qkv_weights, out_weights):
    frames = lax.axis_size("tm")
    local = lax.all_to_all(tokens[0], "space", split_axis=1, concat_axis=0, tiled=True)
    height_n, wide, feat = local.shape
    by_column = jnp.transpose(local, (1, 0, 2))
    done = attend_plain(by_column, gains[0], qkv_weights[0], out_weights[0])
    flat = done.reshape(frames, wide * height_n // frames, feat)
    by_frame = lax.all_to_all(flat, "tm", split_axis=0, concat_axis=0, tiled=True)
    done = attend_plain(
        jnp.transpose(by_frame, (1, 0, 2)), gains[1], qkv_weights[1], out_weights[1]
    )
    back = lax.all_to_all(
        jnp.transpose(done, (1, 0, 2)), "tm", split_axis=0, concat_axis=0, tiled=True
    )
    by_row = jnp.transpose(back.reshape(wide, height_n, feat), (1, 0, 2))
    return lax.all_to_all(by_row, "space", split_axis=0, concat_axis=1, tiled=True)[None]


def solution(mesh):
    frames, pair = mesh.shape["tm"], mesh.shape["space"]
    high = frames // 2

    def shards(tokens, gains, qkv_weights, out_weights):
        _, rows, cols, feat = tokens.shape
        inner = out_weights.shape[1]
        count = rows * cols // CHUNKS
        fits = (
            pair == 2
            and frames == 2 * high
            and high > 1
            and high & (high - 1) == 0
            and cols % (CHUNKS * COLB) == 0
            and count % (high * POSB) == 0
            and inner % (QUAD * HEAD) == 0
            and feat % 128 == 0
        )
        body = fast if fits else plain
        return body(tokens, gains, qkv_weights, out_weights)

    return jax.shard_map(
        shards,
        mesh=mesh,
        in_specs=(P(("grp", "tm"), "space", None, None), P(), P(), P()),
        out_specs=P(("grp", "tm"), "space", None, None),
        check_vma=False,
    )
```

```python
import functools

import jax
import jax.numpy as jnp
from jax import lax
from jax.experimental import pallas as pl
from jax.experimental.pallas import tpu as pltpu
from jax.sharding import PartitionSpec as P


HEAD = 64
EPS = 1e-06
QUAD = 4
CHUNKS = 2
COLB = 8
SPLIT = 4
POSB = 16
NEG = -1e30
VMEM_BYTES = 16 * 1024 * 1024


def params():
    return pltpu.CompilerParams(vmem_limit_bytes=VMEM_BYTES)


def normalise(stream, gain):
    scale = lax.rsqrt(jnp.mean(stream * stream, axis=-1, keepdims=True) + EPS)
    return (stream * scale * gain).astype(jnp.bfloat16)


def group_bias(keys, group):
    left = lax.broadcasted_iota(jnp.int32, (1, group, keys), 1)
    right = lax.broadcasted_iota(jnp.int32, (1, group, keys), 2) % group
    return jnp.where(left == right, 0.0, NEG)


def attend_quad(query, key, value, bias):
    rows, width = query.shape
    keys = key.shape[0]
    lanes = lax.broadcasted_iota(jnp.int32, (rows, width), 1) // HEAD
    heads = width // HEAD
    zero = jnp.zeros_like(query)
    stacked = jnp.concatenate([jnp.where(lanes == h, query, zero) for h in range(heads)], axis=0)
    scores = lax.dot_general(
        stacked, key, (((1,), (1,)), ((), ())), preferred_element_type=jnp.float32
    )
    scores = scores.reshape(heads * rows // bias.shape[1], bias.shape[1], keys) + bias
    raised = jnp.exp(scores - jnp.max(scores, axis=-1, keepdims=True))
    total = jnp.sum(raised, axis=-1, keepdims=True).reshape(heads * rows, 1)
    raised = raised.reshape(heads * rows, keys).astype(jnp.bfloat16)
    mixed = jnp.dot(raised, value, preferred_element_type=jnp.float32) * (1.0 / total)
    out = mixed[:rows]
    for h in range(1, heads):
        out = jnp.where(lanes == h, mixed[h * rows : (h + 1) * rows], out)
    return out.astype(jnp.bfloat16)


def attend(q_ref, kv_ref, other_ref, spans, group, put):
    inner = q_ref.shape[1]
    width = QUAD * HEAD
    keys = 2 * sum(size for _, size in spans[0])
    bias = group_bias(keys, group)

    def rows(ref, span, lo):
        return [ref[at : at + size, lo : lo + width] for at, size in span]

    def join(parts):
        return parts[0] if len(parts) == 1 else jnp.concatenate(parts, axis=0)

    for span in spans:
        for lo in range(0, inner, width):
            key = join(rows(kv_ref, span, lo) + rows(other_ref, span, lo))
            value = join(rows(kv_ref, span, inner + lo) + rows(other_ref, span, inner + lo))
            put(span, lo, attend_quad(join(rows(q_ref, span, lo)), key, value, bias))


def project(normed, w_ref, q_ref, kv_ref, inner):
    kv_ref[...] = jnp.dot(
        normed, w_ref[:, inner:], preferred_element_type=jnp.float32
    ).astype(jnp.bfloat16)
    q_ref[...] = jnp.dot(
        normed, w_ref[:, :inner], preferred_element_type=jnp.float32
    ).astype(jnp.bfloat16) * jnp.bfloat16(HEAD**-0.5)


def load_project_kernel(
    chunks, x_ref, gain_ref, w_ref, q_ref, kv_ref, w_out, gain_out, *refs
):
    x_outs = refs[:chunks]
    x_sem, w_sem, gain_sem = refs[chunks:]
    blocks, rows, colb, feat = x_outs[0].shape
    inner = q_ref.shape[1]
    loads = [
        pltpu.make_async_copy(x_ref.at[:, pl.ds(i * colb, colb), :], x_out.at[b], x_sem.at[i])
        for x_out, i, b in (
            (x_outs[c], c * blocks + b, b) for c in range(chunks) for b in range(blocks)
        )
    ]
    step = feat // SPLIT
    fetches = [
        pltpu.make_async_copy(
            w_ref.at[0, pl.ds(i * step, step), :], w_out.at[pl.ds(i * step, step), :], w_sem.at[i]
        )
        for i in range(SPLIT)
    ]
    gain_load = pltpu.make_async_copy(gain_ref, gain_out, gain_sem)
    for copy in [gain_load] + loads[:blocks] + fetches + loads[blocks:]:
        copy.start()
    gain_load.wait()
    parts = []
    for b in range(blocks):
        loads[b].wait()
        stream = x_outs[0][b].astype(jnp.float32).reshape(rows * colb, feat)
        parts.append(normalise(stream, gain_out[0:1, :]))
    normed = jnp.concatenate(parts, axis=0)
    for fetch in fetches:
        fetch.wait()
    project(normed, w_out, q_ref, kv_ref, inner)
    for load in loads[blocks:]:
        load.wait()


def height_project_kernel(x_ref, gain_ref, w_ref, q_ref, kv_ref):
    blocks, rows, colb, feat = x_ref.shape
    inner = q_ref.shape[1]
    stream = x_ref[...].astype(jnp.float32).reshape(blocks * rows * colb, feat)
    project(normalise(stream, gain_ref[0:1, :]), w_ref, q_ref, kv_ref, inner)


def height_kernel(hi_ref, x_ref, q_ref, kv_ref, other_ref, w_ref, *refs):
    full_ref, mix_ref, w_buf, w_sem = refs[-4:]
    piece_refs = refs[:-4]
    blocks, rows, colb, feat = x_ref.shape
    per = rows * colb
    fetch = pltpu.make_async_copy(w_ref.at[0], w_buf, w_sem)
    fetch.start()

    def put(span, lo, out):
        at, size = span[0]
        mix_ref[at : at + size, lo : lo + out.shape[1]] = out

    attend(q_ref, kv_ref, other_ref, [[(b * per, per)] for b in range(blocks)], colb, put)
    fetch.wait()
    for b in range(blocks):
        stream = x_ref[b].astype(jnp.float32).reshape(per, feat)
        update = jnp.dot(
            mix_ref[b * per : (b + 1) * per, :], w_buf[...], preferred_element_type=jnp.float32
        )
        full_ref[b * per : (b + 1) * per, :] = (stream + update).astype(jnp.bfloat16)
    each = piece_refs[0].shape[0]
    for k, piece_ref in enumerate(piece_refs):
        start = pl.multiple_of(jnp.bitwise_xor(hi_ref[0], k) * each, each)
        piece_ref[...] = full_ref[pl.ds(start, each), :]


def time_project_kernel(*refs):
    gain_ref, w_ref, q_ref, kv_ref = refs[-4:]
    inner = q_ref.shape[1]
    normed = jnp.concatenate(
        [normalise(ref[...].astype(jnp.float32), gain_ref[1:2, :]) for ref in refs[:-4]], axis=0
    )
    project(normed, w_ref, q_ref, kv_ref, inner)


def gate_kernel(in_ref, out_ref):
    out_ref[0] = in_ref[0]


def time_kernel(q_ref, kv_ref, other_ref, *mix_refs):
    each = mix_refs[0].shape[0]
    spans = [
        [(k * each + p, POSB) for k in range(len(mix_refs))] for p in range(0, each, POSB)
    ]

    def put(span, lo, out):
        at = span[0][0]
        for k, ref in enumerate(mix_refs):
            ref[at : at + POSB, lo : lo + out.shape[1]] = out[k * POSB : (k + 1) * POSB]

    attend(q_ref, kv_ref, other_ref, spans, POSB, put)


def finish_kernel(frames, hi_ref, full_ref, w_ref, *refs):
    out_ref, mix_ref = refs[-2:]
    rows, cols, feat = out_ref.shape
    per = rows * COLB
    each = refs[0].shape[0]
    for k in range(frames):
        start = pl.multiple_of(jnp.bitwise_xor(hi_ref[0], k) * each, each)
        mix_ref[pl.ds(start, each), :] = refs[k][...]
    for b in range(cols // COLB):
        update = jnp.dot(
            mix_ref[b * per : (b + 1) * per, :], w_ref[...], preferred_element_type=jnp.float32
        )
        total = full_ref[b * per : (b + 1) * per, :].astype(jnp.float32) + update
        out_ref[:, b * COLB : (b + 1) * COLB, :] = total.reshape(rows, COLB, feat).astype(
            jnp.bfloat16
        )


SMEM = pl.BlockSpec(memory_space=pltpu.SMEM)
HBM = pl.BlockSpec(memory_space=pltpu.HBM)


def cost(flops, moved):
    return pl.CostEstimate(flops=int(flops), bytes_accessed=int(moved), transcendentals=0)


def fast(tokens, gains, qkv_weights, out_weights):
    high = lax.axis_size("tm") // 2
    half = high // 2
    hi = (lax.axis_index("tm") // 2).astype(jnp.int32)[None]
    rows, cols, feat = tokens.shape[1:]
    inner = out_weights.shape[1]
    wide = cols // CHUNKS
    blocks = wide // COLB
    count = rows * wide
    each = count // high
    bf = jnp.bfloat16
    x = pltpu.with_memory_space_constraint(tokens[0], pltpu.HBM)
    gains_far = pltpu.with_memory_space_constraint(gains, pltpu.HBM)
    qkv_far = pltpu.with_memory_space_constraint(qkv_weights, pltpu.HBM)
    out_far = pltpu.with_memory_space_constraint(out_weights, pltpu.HBM)

    def pick(i, n):
        return pl.BlockSpec((None,) + n, lambda _: (i,) + (0,) * len(n))

    def whole(*shape):
        return pl.BlockSpec(shape, lambda _: (0,) * len(shape))

    def call(kernel, flops, **rest):
        return pl.pallas_call(
            kernel,
            grid=(1,),
            compiler_params=params(),
            cost_estimate=cost(flops, 4 * count * feat),
            **rest,
        )

    qkv_out = dict(
        out_specs=[whole(count, inner), whole(count, 2 * inner)],
        out_shape=[
            jax.ShapeDtypeStruct((count, inner), bf),
            jax.ShapeDtypeStruct((count, 2 * inner), bf),
        ],
    )
    qkv_in = [whole(count, inner), whole(count, 2 * inner), whole(count, 2 * inner)]
    work = 2 * count * feat * inner

    def after(values, earlier):
        return lax.optimization_barrier((values, earlier))[0]

    held = (blocks, rows, COLB, feat)
    loaded = [(feat, 3 * inner), gains.shape] + [held] * CHUNKS
    types = [bf, gains.dtype] + [bf] * CHUNKS

    def load_project(x):
        return call(
            functools.partial(load_project_kernel, CHUNKS),
            3 * work,
            in_specs=[HBM, HBM, HBM],
            out_specs=qkv_out["out_specs"] + [whole(*shape) for shape in loaded],
            out_shape=qkv_out["out_shape"]
            + [jax.ShapeDtypeStruct(shape, kind) for shape, kind in zip(loaded, types)],
            scratch_shapes=[
                pltpu.SemaphoreType.DMA((blocks * CHUNKS,)),
                pltpu.SemaphoreType.DMA((SPLIT,)),
                pltpu.SemaphoreType.DMA,
            ],
        )(x, gains_far, qkv_far)

    def height_project(x, gain, weight):
        return call(
            height_project_kernel,
            3 * work,
            in_specs=[whole(*held), whole(*gains.shape), whole(feat, 3 * inner)],
            **qkv_out,
        )(x, gain, weight)

    def height(x, q, kv, other):
        outs = call(
            height_kernel,
            4 * work,
            in_specs=[SMEM, whole(*held)] + qkv_in + [HBM],
            out_specs=[whole(each, feat)] * high + [whole(count, feat)],
            out_shape=[jax.ShapeDtypeStruct((each, feat), bf)] * high
            + [jax.ShapeDtypeStruct((count, feat), bf)],
            scratch_shapes=[
                pltpu.VMEM((count, inner), bf),
                pltpu.VMEM((inner, feat), bf),
                pltpu.SemaphoreType.DMA,
            ],
        )(hi, x, q, kv, other, out_far)
        return outs[:-1], outs[-1]

    def gate(value):
        return pl.pallas_call(
            gate_kernel,
            in_specs=[SMEM],
            out_specs=SMEM,
            out_shape=jax.ShapeDtypeStruct(value.shape, value.dtype),
            compiler_params=params(),
            cost_estimate=cost(1, 8),
            name="gate",
        )(value)

    def time_project(pieces):
        return call(
            time_project_kernel,
            3 * work,
            in_specs=[whole(each, feat)] * high
            + [whole(*gains.shape), pick(1, (feat, 3 * inner))],
            **qkv_out,
        )(*pieces, gains, qkv_weights)

    def timed(q, kv, other):
        return call(
            time_kernel,
            2 * work,
            in_specs=qkv_in,
            out_specs=[whole(each, inner)] * high,
            out_shape=[jax.ShapeDtypeStruct((each, inner), bf)] * high,
        )(q, kv, other)

    def finish(c, hi, full, mixes, prior):
        aliases, extra_specs, extra = {}, [], []
        if prior is not None:
            aliases = {high + 3: 0}
            extra_specs, extra = [pl.BlockSpec(memory_space=pl.ANY)], [prior]
        return call(
            functools.partial(finish_kernel, high),
            work,
            in_specs=[SMEM, whole(count, feat), pick(1, (inner, feat))]
            + [whole(each, inner)] * high
            + extra_specs,
            out_specs=pl.BlockSpec((rows, wide, feat), lambda _: (0, c, 0)),
            out_shape=jax.ShapeDtypeStruct((rows, cols, feat), bf),
            scratch_shapes=[pltpu.VMEM((count, inner), bf)],
            input_output_aliases=aliases,
        )(hi, full, out_weights, *mixes, *extra)

    def swap(a):
        return lax.ppermute(a, "space", [(0, 1), (1, 0)])

    def route(k):
        pairs = []
        for z in range(high):
            for lo in range(2):
                for s in range(2):
                    there = z ^ k
                    to = (there * 2 + (s ^ (there >= half))) * 2 + (lo ^ (z >= half))
                    pairs.append(((z * 2 + lo) * 2 + s, to))
        return pairs

    def permute(piece, k):
        return lax.ppermute(piece, ("tm", "space"), route(k))

    order = list(range(high - 1, -1, -1))

    def exchange(pieces, ks):
        return {k: permute(pieces[k], k) for k in ks}

    q, kv, weight, gain, *xs = load_project(after(x, hi))
    projected, others, heights, arrived, home = [(q, kv)], [], [], [], []
    others.append(swap(kv))
    for c in range(1, CHUNKS):
        projected.append(height_project(after(xs[c], projected[-1][0]), gain, weight))
        others.append(swap(projected[c][1]))
    last = projected[-1][0]
    for c in range(CHUNKS):
        q, kv = projected[c]
        heights.append(height(xs[c], after(q, last), kv, others[c]))
        last = heights[-1][1]
        arrived.append(exchange(heights[-1][0], order))
    heavy, light = order[: high // 2], order[high // 2 :]
    mixes = None
    for c in range(CHUNKS):
        pieces = [arrived[c][k] for k in range(high)]
        q, kv = time_project(after(pieces, last))
        other = swap(kv)
        if mixes is not None:
            mixes = after(mixes, q)
            home[-1].update(exchange(mixes, heavy))
        mixes = timed(q, kv, other)
        last = mixes[0]
        home.append(exchange(mixes, light))
        if c + 1 < CHUNKS:
            hi = gate(after(hi, last))
            last = hi
    home[-1].update(exchange(mixes, heavy))
    out = None
    for c in range(CHUNKS):
        mixes = [home[c][k] for k in range(high)]
        out = finish(c, hi, after(heights[c][1], last), mixes, out)
    return out[None]


def attend_plain(stream, gain, qkv_weight, out_weight):
    groups, length, _ = stream.shape
    inner = out_weight.shape[0]
    heads = inner // HEAD
    wide = stream.astype(jnp.float32)
    normed = normalise(wide, gain)
    projected = jnp.einsum(
        "glf,fe->gle", normed, qkv_weight, preferred_element_type=jnp.float32
    ).astype(jnp.bfloat16)
    q, k, v = jnp.split(projected.reshape(groups, length, 3 * heads, HEAD), 3, axis=2)
    scores = jnp.einsum("gqhd,gkhd->ghqk", q, k, preferred_element_type=jnp.float32) * HEAD**-0.5
    weights = jax.nn.softmax(scores, axis=-1).astype(jnp.bfloat16)
    mixture = jnp.einsum("ghqk,gkhd->gqhd", weights, v, preferred_element_type=jnp.float32)
    mixture = mixture.astype(jnp.bfloat16).reshape(groups, length, inner)
    update = jnp.einsum("gle,ef->glf", mixture, out_weight, preferred_element_type=jnp.float32)
    return (wide + update).astype(jnp.bfloat16)


def plain(tokens, gains, qkv_weights, out_weights):
    frames = lax.axis_size("tm")
    local = lax.all_to_all(tokens[0], "space", split_axis=1, concat_axis=0, tiled=True)
    height_n, wide, feat = local.shape
    by_column = jnp.transpose(local, (1, 0, 2))
    done = attend_plain(by_column, gains[0], qkv_weights[0], out_weights[0])
    flat = done.reshape(frames, wide * height_n // frames, feat)
    by_frame = lax.all_to_all(flat, "tm", split_axis=0, concat_axis=0, tiled=True)
    done = attend_plain(
        jnp.transpose(by_frame, (1, 0, 2)), gains[1], qkv_weights[1], out_weights[1]
    )
    back = lax.all_to_all(
        jnp.transpose(done, (1, 0, 2)), "tm", split_axis=0, concat_axis=0, tiled=True
    )
    by_row = jnp.transpose(back.reshape(wide, height_n, feat), (1, 0, 2))
    return lax.all_to_all(by_row, "space", split_axis=0, concat_axis=1, tiled=True)[None]


def solution(mesh):
    frames, pair = mesh.shape["tm"], mesh.shape["space"]
    high = frames // 2

    def shards(tokens, gains, qkv_weights, out_weights):
        _, rows, cols, feat = tokens.shape
        inner = out_weights.shape[1]
        count = rows * cols // CHUNKS
        fits = (
            pair == 2
            and frames == 2 * high
            and high > 1
            and high & (high - 1) == 0
            and cols % (CHUNKS * COLB) == 0
            and count % (high * POSB) == 0
            and inner % (QUAD * HEAD) == 0
            and feat % 128 == 0
        )
        body = fast if fits else plain
        return body(tokens, gains, qkv_weights, out_weights)

    return jax.shard_map(
        shards,
        mesh=mesh,
        in_specs=(P(("grp", "tm"), "space", None, None), P(), P(), P()),
        out_specs=P(("grp", "tm"), "space", None, None),
        check_vma=False,
    )
```

```python
import functools

import jax
import jax.numpy as jnp
from jax import lax
from jax.experimental import pallas as pl
from jax.experimental.pallas import tpu as pltpu
from jax.sharding import PartitionSpec as P


HEAD = 64
EPS = 1e-06
QUAD = 4
CHUNKS = 2
COLB = 8
SPLIT = 4
POSB = 16
NEG = -1e30
VMEM_BYTES = 16 * 1024 * 1024


def params():
    return pltpu.CompilerParams(vmem_limit_bytes=VMEM_BYTES)


def normalise(stream, gain):
    scale = lax.rsqrt(jnp.mean(stream * stream, axis=-1, keepdims=True) + EPS)
    return (stream * scale * gain).astype(jnp.bfloat16)


def group_bias(keys, group):
    left = lax.broadcasted_iota(jnp.int32, (1, group, keys), 1)
    right = lax.broadcasted_iota(jnp.int32, (1, group, keys), 2) % group
    return jnp.where(left == right, 0.0, NEG)


def attend_quad(query, key, value, bias):
    rows, width = query.shape
    keys = key.shape[0]
    lanes = lax.broadcasted_iota(jnp.int32, (rows, width), 1) // HEAD
    heads = width // HEAD
    zero = jnp.zeros_like(query)
    stacked = jnp.concatenate([jnp.where(lanes == h, query, zero) for h in range(heads)], axis=0)
    scores = lax.dot_general(
        stacked, key, (((1,), (1,)), ((), ())), preferred_element_type=jnp.float32
    )
    scores = scores.reshape(heads * rows // bias.shape[1], bias.shape[1], keys) + bias
    raised = jnp.exp(scores - jnp.max(scores, axis=-1, keepdims=True))
    total = jnp.sum(raised, axis=-1, keepdims=True).reshape(heads * rows, 1)
    raised = raised.reshape(heads * rows, keys).astype(jnp.bfloat16)
    mixed = jnp.dot(raised, value, preferred_element_type=jnp.float32) * (1.0 / total)
    out = mixed[:rows]
    for h in range(1, heads):
        out = jnp.where(lanes == h, mixed[h * rows : (h + 1) * rows], out)
    return out.astype(jnp.bfloat16)


def attend(q_ref, kv_ref, other_ref, spans, group, put):
    inner = q_ref.shape[1]
    width = QUAD * HEAD
    keys = 2 * sum(size for _, size in spans[0])
    bias = group_bias(keys, group)

    def rows(ref, span, lo):
        return [ref[at : at + size, lo : lo + width] for at, size in span]

    def join(parts):
        return parts[0] if len(parts) == 1 else jnp.concatenate(parts, axis=0)

    for span in spans:
        for lo in range(0, inner, width):
            key = join(rows(kv_ref, span, lo) + rows(other_ref, span, lo))
            value = join(rows(kv_ref, span, inner + lo) + rows(other_ref, span, inner + lo))
            put(span, lo, attend_quad(join(rows(q_ref, span, lo)), key, value, bias))


def project_keys(normed, w_ref, kv_ref):
    inner = kv_ref.shape[1] // 2
    kv_ref[...] = jnp.dot(
        normed, w_ref[:, inner:], preferred_element_type=jnp.float32
    ).astype(jnp.bfloat16)


def project_queries(normed, w_ref, q_ref):
    q_ref[...] = jnp.dot(
        normed, w_ref[:, : q_ref.shape[1]], preferred_element_type=jnp.float32
    ).astype(jnp.bfloat16) * jnp.bfloat16(HEAD**-0.5)


def load_kernel(x_ref, gain_ref, w_ref, kv_ref, normed_ref, w_out, gain_out, *refs):
    x_outs, (x_sem, w_sem, gain_sem) = refs[:CHUNKS], refs[CHUNKS:]
    blocks, rows, colb, feat = x_outs[0].shape
    inner = kv_ref.shape[1] // 2
    loads = [
        pltpu.make_async_copy(
            x_ref.at[:, pl.ds((c * blocks + b) * colb, colb), :],
            x_outs[c].at[b],
            x_sem.at[c * blocks + b],
        )
        for c in range(CHUNKS)
        for b in range(blocks)
    ]
    step = feat // SPLIT
    fetches = [
        pltpu.make_async_copy(
            w_ref.at[0, pl.ds(i * step, step), :], w_out.at[pl.ds(i * step, step), :], w_sem.at[i]
        )
        for i in range(SPLIT)
    ]
    gain_load = pltpu.make_async_copy(gain_ref, gain_out, gain_sem)
    for copy in [gain_load] + loads[:blocks] + fetches + loads[blocks:]:
        copy.start()
    gain_load.wait()
    per = rows * colb
    for b in range(blocks):
        loads[b].wait()
        stream = x_outs[0][b].astype(jnp.float32).reshape(per, feat)
        normed_ref[b * per : (b + 1) * per, :] = normalise(stream, gain_out[0:1, :])
    total = None
    for i, fetch in enumerate(fetches):
        fetch.wait()
        span = slice(i * step, (i + 1) * step)
        part = jnp.dot(
            normed_ref[:, span], w_out[span, inner:], preferred_element_type=jnp.float32
        )
        total = part if total is None else total + part
    kv_ref[...] = total.astype(jnp.bfloat16)
    for load in loads[blocks:]:
        load.wait()


def second_kernel(first_ref, x_ref, gain_ref, w_ref, q0_ref, q_ref, kv_ref):
    blocks, rows, colb, feat = x_ref.shape
    stream = x_ref[...].astype(jnp.float32).reshape(blocks * rows * colb, feat)
    normed = normalise(stream, gain_ref[0:1, :])
    project_keys(normed, w_ref, kv_ref)
    project_queries(first_ref[...], w_ref, q0_ref)
    project_queries(normed, w_ref, q_ref)


def height_kernel(ks, hi_ref, x_ref, q_ref, kv_ref, other_ref, w_ref, *refs):
    mix_ref, w_buf, w_sem = refs[-3:]
    _, rows, colb, feat = x_ref.shape
    per = rows * colb
    fetch = pltpu.make_async_copy(w_ref.at[0], w_buf, w_sem)
    fetch.start()
    inner = q_ref.shape[1]
    width = QUAD * HEAD
    bias = group_bias(2 * per, colb)
    places = [jnp.bitwise_xor(hi_ref[0], k) for k in ks]
    for i, place in enumerate(places):
        span = pl.ds(pl.multiple_of(place * per, per), per)
        for lo in range(0, inner, width):
            here, there = slice(lo, lo + width), slice(inner + lo, inner + lo + width)
            key = jnp.concatenate([kv_ref[span, here], other_ref[span, here]], axis=0)
            value = jnp.concatenate([kv_ref[span, there], other_ref[span, there]], axis=0)
            mix_ref[i * per : (i + 1) * per, here] = attend_quad(
                q_ref[span, here], key, value, bias
            )
    fetch.wait()
    update = jnp.dot(mix_ref[...], w_buf[...], preferred_element_type=jnp.float32)
    for i, place in enumerate(places):
        stream = x_ref[place].astype(jnp.float32).reshape(per, feat)
        refs[i][...] = (stream + update[i * per : (i + 1) * per]).astype(jnp.bfloat16)


def time_project_kernel(*refs):
    gain_ref, w_ref, q_ref, kv_ref = refs[-4:]
    normed = jnp.concatenate(
        [normalise(ref[...].astype(jnp.float32), gain_ref[1:2, :]) for ref in refs[:-4]], axis=0
    )
    project_keys(normed, w_ref, kv_ref)
    project_queries(normed, w_ref, q_ref)


def gate_kernel(in_ref, out_ref):
    out_ref[0] = in_ref[0]


def time_kernel(q_ref, kv_ref, other_ref, *mix_refs):
    each = mix_refs[0].shape[0]
    spans = [
        [(k * each + p, POSB) for k in range(len(mix_refs))] for p in range(0, each, POSB)
    ]

    def put(span, lo, out):
        at = span[0][0]
        for k, ref in enumerate(mix_refs):
            ref[at : at + POSB, lo : lo + out.shape[1]] = out[k * POSB : (k + 1) * POSB]

    attend(q_ref, kv_ref, other_ref, spans, POSB, put)


def finish_kernel(c, high, hi_ref, w_ref, *refs):
    pieces, mixes = refs[:high], refs[high : 2 * high]
    out_ref, buf, sem = refs[-3:]
    _, rows, colb, feat = buf.shape
    per = rows * colb
    mixed = jnp.concatenate([ref[...] for ref in mixes], axis=0)
    update = jnp.dot(mixed, w_ref[...], preferred_element_type=jnp.float32)
    copies = []
    for k in range(high):
        total = pieces[k][...].astype(jnp.float32) + update[k * per : (k + 1) * per]
        buf[k] = total.reshape(rows, colb, feat).astype(jnp.bfloat16)
        place = c * high + jnp.bitwise_xor(hi_ref[0], k)
        column = pl.multiple_of(place * colb, colb)
        copies.append(
            pltpu.make_async_copy(buf.at[k], out_ref.at[:, pl.ds(column, colb), :], sem.at[k])
        )
        copies[-1].start()
    for copy in copies:
        copy.wait()


SMEM = pl.BlockSpec(memory_space=pltpu.SMEM)
HBM = pl.BlockSpec(memory_space=pltpu.HBM)


def cost(flops, moved):
    return pl.CostEstimate(flops=int(flops), bytes_accessed=int(moved), transcendentals=0)


def fast(tokens, gains, qkv_weights, out_weights):
    high = lax.axis_size("tm") // 2
    half = high // 2
    hi = (lax.axis_index("tm") // 2).astype(jnp.int32)[None]
    rows, cols, feat = tokens.shape[1:]
    inner = out_weights.shape[1]
    wide = cols // CHUNKS
    blocks = wide // COLB
    count = rows * wide
    each = count // high
    bf = jnp.bfloat16
    x = pltpu.with_memory_space_constraint(tokens[0], pltpu.HBM)
    gains_far = pltpu.with_memory_space_constraint(gains, pltpu.HBM)
    qkv_far = pltpu.with_memory_space_constraint(qkv_weights, pltpu.HBM)
    out_far = pltpu.with_memory_space_constraint(out_weights, pltpu.HBM)

    def pick(i, n):
        return pl.BlockSpec((None,) + n, lambda _: (i,) + (0,) * len(n))

    def whole(*shape):
        return pl.BlockSpec(shape, lambda _: (0,) * len(shape))

    def call(kernel, flops, **rest):
        return pl.pallas_call(
            kernel,
            grid=(1,),
            compiler_params=params(),
            cost_estimate=cost(flops, 4 * count * feat),
            **rest,
        )

    qkv_out = dict(
        out_specs=[whole(count, inner), whole(count, 2 * inner)],
        out_shape=[
            jax.ShapeDtypeStruct((count, inner), bf),
            jax.ShapeDtypeStruct((count, 2 * inner), bf),
        ],
    )
    qkv_in = [whole(count, inner), whole(count, 2 * inner), whole(count, 2 * inner)]
    work = 2 * count * feat * inner

    def after(values, earlier):
        return lax.optimization_barrier((values, earlier))[0]

    held = (blocks, rows, COLB, feat)

    def load(x):
        shapes = [(count, 2 * inner), (count, feat), (feat, 3 * inner), gains.shape]
        shapes += [held] * CHUNKS
        kinds = [bf, bf, bf, gains.dtype] + [bf] * CHUNKS
        return call(
            load_kernel,
            2 * work,
            in_specs=[HBM, HBM, HBM],
            out_specs=[whole(*shape) for shape in shapes],
            out_shape=[jax.ShapeDtypeStruct(*pair) for pair in zip(shapes, kinds)],
            scratch_shapes=[
                pltpu.SemaphoreType.DMA((blocks * CHUNKS,)),
                pltpu.SemaphoreType.DMA((SPLIT,)),
                pltpu.SemaphoreType.DMA,
            ],
        )(x, gains_far, qkv_far)

    def second(first, x, gain, weight):
        return call(
            second_kernel,
            4 * work,
            in_specs=[
                whole(count, feat),
                whole(*held),
                whole(*gains.shape),
                whole(feat, 3 * inner),
            ],
            out_specs=[whole(count, inner)] + qkv_out["out_specs"],
            out_shape=[jax.ShapeDtypeStruct((count, inner), bf)] + qkv_out["out_shape"],
        )(first, x, gain, weight)

    def height(ks, x, q, kv, other):
        return call(
            functools.partial(height_kernel, ks),
            2 * work,
            in_specs=[SMEM, whole(*held)] + qkv_in + [HBM],
            out_specs=[whole(each, feat)] * len(ks),
            out_shape=[jax.ShapeDtypeStruct((each, feat), bf)] * len(ks),
            scratch_shapes=[
                pltpu.VMEM((len(ks) * each, inner), bf),
                pltpu.VMEM((inner, feat), bf),
                pltpu.SemaphoreType.DMA,
            ],
        )(hi, x, q, kv, other, out_far)

    def gate(value):
        return pl.pallas_call(
            gate_kernel,
            in_specs=[SMEM],
            out_specs=SMEM,
            out_shape=jax.ShapeDtypeStruct(value.shape, value.dtype),
            compiler_params=params(),
            cost_estimate=cost(1, 8),
            name="gate",
        )(value)

    def time_project(pieces):
        return call(
            time_project_kernel,
            3 * work,
            in_specs=[whole(each, feat)] * high
            + [whole(*gains.shape), pick(1, (feat, 3 * inner))],
            **qkv_out,
        )(*pieces, gains, qkv_weights)

    def timed(q, kv, other):
        return call(
            time_kernel,
            2 * work,
            in_specs=qkv_in,
            out_specs=[whole(each, inner)] * high,
            out_shape=[jax.ShapeDtypeStruct((each, inner), bf)] * high,
        )(q, kv, other)

    def finish(c, hi, pieces, mixes, prior):
        extra_specs, extra = [], []
        if prior is not None:
            extra_specs, extra = [pl.BlockSpec(memory_space=pl.ANY)], [prior]
        return call(
            functools.partial(finish_kernel, c, high),
            work,
            in_specs=[SMEM, pick(1, (inner, feat))]
            + [whole(each, feat)] * high
            + [whole(each, inner)] * high
            + extra_specs,
            out_specs=HBM,
            out_shape=jax.ShapeDtypeStruct((rows, cols, feat), bf),
            scratch_shapes=[pltpu.VMEM(held, bf), pltpu.SemaphoreType.DMA((high,))],
            input_output_aliases={2 * high + 2: 0} if extra else {},
        )(hi, out_weights, *pieces, *mixes, *extra)

    def swap(a):
        return lax.ppermute(a, "space", [(0, 1), (1, 0)])

    def route(k):
        pairs = []
        for z in range(high):
            for lo in range(2):
                for s in range(2):
                    there = z ^ k
                    to = (there * 2 + (s ^ (there >= half))) * 2 + (lo ^ (z >= half))
                    pairs.append(((z * 2 + lo) * 2 + s, to))
        return pairs

    def permute(piece, k):
        return lax.ppermute(piece, ("tm", "space"), route(k))

    order = list(range(high - 1, -1, -1))
    heavy, light = order[:half], order[half:]

    def exchange(pieces, ks):
        return {k: permute(pieces[k], k) for k in ks}

    kv, first, weight, gain, *xs = load(after(x, hi))
    others = [swap(kv)]
    q0, q1, kv1 = second(first, xs[1], gain, weight)
    others.append(swap(kv1))
    queries, keys = [q0, q1], [kv, kv1]
    pieces, arrived, home = [], [], []
    last = q1
    for c in range(CHUNKS):
        made, got = {}, {}
        for name, ks in (("far", heavy), ("near", light)):
            q = after(queries[c], last)
            outs = height(ks, xs[c], q, keys[c], others[c])
            last = outs[0]
            made.update(zip(ks, outs))
            ready = dict(made)
            if c and name == "far":
                ready[heavy[-1]] = after(made[heavy[-1]], arrived[-1][heavy[-1]])
            got.update(exchange(ready, ks))
        pieces.append(made)
        arrived.append(got)
    mixes = None
    for c in range(CHUNKS):
        got = [arrived[c][k] for k in range(high)]
        q, kv = time_project(after(got, last))
        other = swap(kv)
        if mixes is not None:
            mixes = after(mixes, q)
            home[-1].update(exchange(mixes, heavy))
        mixes = timed(q, kv, other)
        last = mixes[0]
        home.append(exchange(mixes, light))
        if c + 1 < CHUNKS:
            hi = gate(after(hi, last))
            last = hi
    home[-1].update(exchange(mixes, heavy))
    out = None
    for c in range(CHUNKS):
        made = after([pieces[c][k] for k in range(high)], last)
        mixes = [home[c][k] for k in range(high)]
        out = finish(c, hi, made, mixes, out)
    return out[None]


def attend_plain(stream, gain, qkv_weight, out_weight):
    groups, length, _ = stream.shape
    inner = out_weight.shape[0]
    heads = inner // HEAD
    wide = stream.astype(jnp.float32)
    normed = normalise(wide, gain)
    projected = jnp.einsum(
        "glf,fe->gle", normed, qkv_weight, preferred_element_type=jnp.float32
    ).astype(jnp.bfloat16)
    q, k, v = jnp.split(projected.reshape(groups, length, 3 * heads, HEAD), 3, axis=2)
    scores = jnp.einsum("gqhd,gkhd->ghqk", q, k, preferred_element_type=jnp.float32) * HEAD**-0.5
    weights = jax.nn.softmax(scores, axis=-1).astype(jnp.bfloat16)
    mixture = jnp.einsum("ghqk,gkhd->gqhd", weights, v, preferred_element_type=jnp.float32)
    mixture = mixture.astype(jnp.bfloat16).reshape(groups, length, inner)
    update = jnp.einsum("gle,ef->glf", mixture, out_weight, preferred_element_type=jnp.float32)
    return (wide + update).astype(jnp.bfloat16)


def plain(tokens, gains, qkv_weights, out_weights):
    frames = lax.axis_size("tm")
    local = lax.all_to_all(tokens[0], "space", split_axis=1, concat_axis=0, tiled=True)
    height_n, wide, feat = local.shape
    by_column = jnp.transpose(local, (1, 0, 2))
    done = attend_plain(by_column, gains[0], qkv_weights[0], out_weights[0])
    flat = done.reshape(frames, wide * height_n // frames, feat)
    by_frame = lax.all_to_all(flat, "tm", split_axis=0, concat_axis=0, tiled=True)
    done = attend_plain(
        jnp.transpose(by_frame, (1, 0, 2)), gains[1], qkv_weights[1], out_weights[1]
    )
    back = lax.all_to_all(
        jnp.transpose(done, (1, 0, 2)), "tm", split_axis=0, concat_axis=0, tiled=True
    )
    by_row = jnp.transpose(back.reshape(wide, height_n, feat), (1, 0, 2))
    return lax.all_to_all(by_row, "space", split_axis=0, concat_axis=1, tiled=True)[None]


def solution(mesh):
    frames, pair = mesh.shape["tm"], mesh.shape["space"]
    high = frames // 2

    def shards(tokens, gains, qkv_weights, out_weights):
        _, rows, cols, feat = tokens.shape
        inner = out_weights.shape[1]
        count = rows * cols // CHUNKS
        fits = (
            pair == 2
            and frames == 2 * high
            and high > 1
            and high & (high - 1) == 0
            and cols == CHUNKS * COLB * high
            and count % (high * POSB) == 0
            and inner % (QUAD * HEAD) == 0
            and feat % 128 == 0
        )
        body = fast if fits else plain
        return body(tokens, gains, qkv_weights, out_weights)

    return jax.shard_map(
        shards,
        mesh=mesh,
        in_specs=(P(("grp", "tm"), "space", None, None), P(), P(), P()),
        out_specs=P(("grp", "tm"), "space", None, None),
        check_vma=False,
    )
```

```python
import functools

import jax
import jax.numpy as jnp
from jax import lax
from jax.experimental import pallas as pl
from jax.experimental.pallas import tpu as pltpu
from jax.sharding import PartitionSpec as P


HEAD = 64
EPS = 1e-06
QUAD = 4
CHUNKS = 2
COLB = 8
SPLIT = 4
POSB = 16
NEG = -1e30
VMEM_BYTES = 16 * 1024 * 1024


def params():
    return pltpu.CompilerParams(vmem_limit_bytes=VMEM_BYTES)


def normalise(stream, gain):
    scale = lax.rsqrt(jnp.mean(stream * stream, axis=-1, keepdims=True) + EPS)
    return (stream * scale * gain).astype(jnp.bfloat16)


def group_bias(keys, group):
    left = lax.broadcasted_iota(jnp.int32, (1, group, keys), 1)
    right = lax.broadcasted_iota(jnp.int32, (1, group, keys), 2) % group
    return jnp.where(left == right, 0.0, NEG)


def attend_quad(query, key, value, bias):
    rows, width = query.shape
    keys = key.shape[0]
    lanes = lax.broadcasted_iota(jnp.int32, (rows, width), 1) // HEAD
    heads = width // HEAD
    zero = jnp.zeros_like(query)
    stacked = jnp.concatenate([jnp.where(lanes == h, query, zero) for h in range(heads)], axis=0)
    scores = lax.dot_general(
        stacked, key, (((1,), (1,)), ((), ())), preferred_element_type=jnp.float32
    )
    scores = scores.reshape(heads * rows // bias.shape[1], bias.shape[1], keys) + bias
    raised = jnp.exp(scores - jnp.max(scores, axis=-1, keepdims=True))
    total = jnp.sum(raised, axis=-1, keepdims=True).reshape(heads * rows, 1)
    raised = raised.reshape(heads * rows, keys).astype(jnp.bfloat16)
    mixed = jnp.dot(raised, value, preferred_element_type=jnp.float32) * (1.0 / total)
    out = mixed[:rows]
    for h in range(1, heads):
        out = jnp.where(lanes == h, mixed[h * rows : (h + 1) * rows], out)
    return out.astype(jnp.bfloat16)


def attend(q_ref, kv_ref, other_ref, spans, group, put):
    inner = q_ref.shape[1]
    width = QUAD * HEAD
    keys = 2 * sum(size for _, size in spans[0])
    bias = group_bias(keys, group)

    def rows(ref, span, lo):
        return [ref[at : at + size, lo : lo + width] for at, size in span]

    def join(parts):
        return parts[0] if len(parts) == 1 else jnp.concatenate(parts, axis=0)

    for span in spans:
        for lo in range(0, inner, width):
            key = join(rows(kv_ref, span, lo) + rows(other_ref, span, lo))
            value = join(rows(kv_ref, span, inner + lo) + rows(other_ref, span, inner + lo))
            put(span, lo, attend_quad(join(rows(q_ref, span, lo)), key, value, bias))


def project_keys(normed, w_ref, kv_ref):
    inner = kv_ref.shape[1] // 2
    kv_ref[...] = jnp.dot(
        normed, w_ref[:, inner:], preferred_element_type=jnp.float32
    ).astype(jnp.bfloat16)


def project_queries(normed, w_ref, q_ref):
    q_ref[...] = jnp.dot(
        normed, w_ref[:, : q_ref.shape[1]], preferred_element_type=jnp.float32
    ).astype(jnp.bfloat16) * jnp.bfloat16(HEAD**-0.5)


def load_kernel(x_ref, gain_ref, w_ref, kv_ref, normed_ref, w_out, gain_out, *refs):
    x_outs, (x_sem, w_sem, gain_sem) = refs[:CHUNKS], refs[CHUNKS:]
    blocks, rows, colb, feat = x_outs[0].shape
    inner = kv_ref.shape[1] // 2
    loads = [
        pltpu.make_async_copy(
            x_ref.at[:, pl.ds((c * blocks + b) * colb, colb), :],
            x_outs[c].at[b],
            x_sem.at[c * blocks + b],
        )
        for c in range(CHUNKS)
        for b in range(blocks)
    ]
    step = feat // SPLIT
    fetches = [
        pltpu.make_async_copy(
            w_ref.at[0, pl.ds(i * step, step), :], w_out.at[pl.ds(i * step, step), :], w_sem.at[i]
        )
        for i in range(SPLIT)
    ]
    gain_load = pltpu.make_async_copy(gain_ref, gain_out, gain_sem)
    for copy in [gain_load] + loads[:blocks] + fetches + loads[blocks:]:
        copy.start()
    gain_load.wait()
    per = rows * colb
    for b in range(blocks):
        loads[b].wait()
        stream = x_outs[0][b].astype(jnp.float32).reshape(per, feat)
        normed_ref[b * per : (b + 1) * per, :] = normalise(stream, gain_out[0:1, :])
    total = None
    for i, fetch in enumerate(fetches):
        fetch.wait()
        span = slice(i * step, (i + 1) * step)
        part = jnp.dot(
            normed_ref[:, span], w_out[span, inner:], preferred_element_type=jnp.float32
        )
        total = part if total is None else total + part
    kv_ref[...] = total.astype(jnp.bfloat16)
    for load in loads[blocks:]:
        load.wait()


def second_kernel(first_ref, x_ref, gain_ref, w_ref, q0_ref, q_ref, kv_ref):
    blocks, rows, colb, feat = x_ref.shape
    stream = x_ref[...].astype(jnp.float32).reshape(blocks * rows * colb, feat)
    normed = normalise(stream, gain_ref[0:1, :])
    project_keys(normed, w_ref, kv_ref)
    project_queries(first_ref[...], w_ref, q0_ref)
    project_queries(normed, w_ref, q_ref)


def height_kernel(ks, hi_ref, x_ref, q_ref, kv_ref, other_ref, w_ref, *refs):
    mix_ref, w_buf, w_sem = refs[-3:]
    _, rows, colb, feat = x_ref.shape
    per = rows * colb
    fetch = pltpu.make_async_copy(w_ref.at[0], w_buf, w_sem)
    fetch.start()
    inner = q_ref.shape[1]
    width = QUAD * HEAD
    bias = group_bias(2 * per, colb)
    places = [jnp.bitwise_xor(hi_ref[0], k) for k in ks]
    for i, place in enumerate(places):
        span = pl.ds(pl.multiple_of(place * per, per), per)
        for lo in range(0, inner, width):
            here, there = slice(lo, lo + width), slice(inner + lo, inner + lo + width)
            key = jnp.concatenate([kv_ref[span, here], other_ref[span, here]], axis=0)
            value = jnp.concatenate([kv_ref[span, there], other_ref[span, there]], axis=0)
            mix_ref[i * per : (i + 1) * per, here] = attend_quad(
                q_ref[span, here], key, value, bias
            )
    fetch.wait()
    update = jnp.dot(mix_ref[...], w_buf[...], preferred_element_type=jnp.float32)
    for i, place in enumerate(places):
        stream = x_ref[place].astype(jnp.float32).reshape(per, feat)
        refs[i][...] = (stream + update[i * per : (i + 1) * per]).astype(jnp.bfloat16)


def time_project_kernel(*refs):
    gain_ref, w_ref, q_ref, kv_ref = refs[-4:]
    normed = jnp.concatenate(
        [normalise(ref[...].astype(jnp.float32), gain_ref[1:2, :]) for ref in refs[:-4]], axis=0
    )
    project_keys(normed, w_ref, kv_ref)
    project_queries(normed, w_ref, q_ref)


def gate_kernel(in_ref, out_ref):
    out_ref[0] = in_ref[0]


def time_kernel(q_ref, kv_ref, other_ref, *mix_refs):
    each = mix_refs[0].shape[0]
    spans = [
        [(k * each + p, POSB) for k in range(len(mix_refs))] for p in range(0, each, POSB)
    ]

    def put(span, lo, out):
        at = span[0][0]
        for k, ref in enumerate(mix_refs):
            ref[at : at + POSB, lo : lo + out.shape[1]] = out[k * POSB : (k + 1) * POSB]

    attend(q_ref, kv_ref, other_ref, spans, POSB, put)


def finish_kernel(c, ks, high, hi_ref, w_ref, *refs):
    pieces, mixes = refs[: len(ks)], refs[len(ks) : 2 * len(ks)]
    out_ref, buf, sem = refs[-3:]
    _, rows, colb, feat = buf.shape
    per = rows * colb
    mixed = jnp.concatenate([ref[...] for ref in mixes], axis=0)
    update = jnp.dot(mixed, w_ref[...], preferred_element_type=jnp.float32)
    copies = []
    for i, k in enumerate(ks):
        total = pieces[i][...].astype(jnp.float32) + update[i * per : (i + 1) * per]
        buf[i] = total.reshape(rows, colb, feat).astype(jnp.bfloat16)
        place = c * high + jnp.bitwise_xor(hi_ref[0], k)
        column = pl.multiple_of(place * colb, colb)
        copies.append(
            pltpu.make_async_copy(buf.at[i], out_ref.at[:, pl.ds(column, colb), :], sem.at[i])
        )
        copies[-1].start()
    for copy in copies:
        copy.wait()


SMEM = pl.BlockSpec(memory_space=pltpu.SMEM)
HBM = pl.BlockSpec(memory_space=pltpu.HBM)


def cost(flops, moved):
    return pl.CostEstimate(flops=int(flops), bytes_accessed=int(moved), transcendentals=0)


def fast(tokens, gains, qkv_weights, out_weights):
    high = lax.axis_size("tm") // 2
    half = high // 2
    hi = (lax.axis_index("tm") // 2).astype(jnp.int32)[None]
    rows, cols, feat = tokens.shape[1:]
    inner = out_weights.shape[1]
    wide = cols // CHUNKS
    blocks = wide // COLB
    count = rows * wide
    each = count // high
    bf = jnp.bfloat16
    x = pltpu.with_memory_space_constraint(tokens[0], pltpu.HBM)
    gains_far = pltpu.with_memory_space_constraint(gains, pltpu.HBM)
    qkv_far = pltpu.with_memory_space_constraint(qkv_weights, pltpu.HBM)
    out_far = pltpu.with_memory_space_constraint(out_weights, pltpu.HBM)

    def pick(i, n):
        return pl.BlockSpec((None,) + n, lambda _: (i,) + (0,) * len(n))

    def whole(*shape):
        return pl.BlockSpec(shape, lambda _: (0,) * len(shape))

    def call(kernel, flops, **rest):
        return pl.pallas_call(
            kernel,
            grid=(1,),
            compiler_params=params(),
            cost_estimate=cost(flops, 4 * count * feat),
            **rest,
        )

    qkv_out = dict(
        out_specs=[whole(count, inner), whole(count, 2 * inner)],
        out_shape=[
            jax.ShapeDtypeStruct((count, inner), bf),
            jax.ShapeDtypeStruct((count, 2 * inner), bf),
        ],
    )
    qkv_in = [whole(count, inner), whole(count, 2 * inner), whole(count, 2 * inner)]
    work = 2 * count * feat * inner

    def after(values, earlier):
        return lax.optimization_barrier((values, earlier))[0]

    held = (blocks, rows, COLB, feat)

    def load(x):
        shapes = [(count, 2 * inner), (count, feat), (feat, 3 * inner), gains.shape]
        shapes += [held] * CHUNKS
        kinds = [bf, bf, bf, gains.dtype] + [bf] * CHUNKS
        return call(
            load_kernel,
            2 * work,
            in_specs=[HBM, HBM, HBM],
            out_specs=[whole(*shape) for shape in shapes],
            out_shape=[jax.ShapeDtypeStruct(*pair) for pair in zip(shapes, kinds)],
            scratch_shapes=[
                pltpu.SemaphoreType.DMA((blocks * CHUNKS,)),
                pltpu.SemaphoreType.DMA((SPLIT,)),
                pltpu.SemaphoreType.DMA,
            ],
        )(x, gains_far, qkv_far)

    def second(first, x, gain, weight):
        return call(
            second_kernel,
            4 * work,
            in_specs=[
                whole(count, feat),
                whole(*held),
                whole(*gains.shape),
                whole(feat, 3 * inner),
            ],
            out_specs=[whole(count, inner)] + qkv_out["out_specs"],
            out_shape=[jax.ShapeDtypeStruct((count, inner), bf)] + qkv_out["out_shape"],
        )(first, x, gain, weight)

    def height(ks, x, q, kv, other):
        return call(
            functools.partial(height_kernel, ks),
            2 * work,
            in_specs=[SMEM, whole(*held)] + qkv_in + [HBM],
            out_specs=[whole(each, feat)] * len(ks),
            out_shape=[jax.ShapeDtypeStruct((each, feat), bf)] * len(ks),
            scratch_shapes=[
                pltpu.VMEM((len(ks) * each, inner), bf),
                pltpu.VMEM((inner, feat), bf),
                pltpu.SemaphoreType.DMA,
            ],
        )(hi, x, q, kv, other, out_far)

    def gate(value):
        return pl.pallas_call(
            gate_kernel,
            in_specs=[SMEM],
            out_specs=SMEM,
            out_shape=jax.ShapeDtypeStruct(value.shape, value.dtype),
            compiler_params=params(),
            cost_estimate=cost(1, 8),
            name="gate",
        )(value)

    def time_project(pieces):
        return call(
            time_project_kernel,
            3 * work,
            in_specs=[whole(each, feat)] * high
            + [whole(*gains.shape), pick(1, (feat, 3 * inner))],
            **qkv_out,
        )(*pieces, gains, qkv_weights)

    def timed(q, kv, other):
        return call(
            time_kernel,
            2 * work,
            in_specs=qkv_in,
            out_specs=[whole(each, inner)] * high,
            out_shape=[jax.ShapeDtypeStruct((each, inner), bf)] * high,
        )(q, kv, other)

    def finish(c, ks, hi, pieces, mixes, prior):
        extra_specs, extra = [], []
        if prior is not None:
            extra_specs, extra = [pl.BlockSpec(memory_space=pl.ANY)], [prior]
        return call(
            functools.partial(finish_kernel, c, ks, high),
            work // 2,
            in_specs=[SMEM, pick(1, (inner, feat))]
            + [whole(each, feat)] * len(ks)
            + [whole(each, inner)] * len(ks)
            + extra_specs,
            out_specs=HBM,
            out_shape=jax.ShapeDtypeStruct((rows, cols, feat), bf),
            scratch_shapes=[
                pltpu.VMEM((len(ks), rows, COLB, feat), bf),
                pltpu.SemaphoreType.DMA((len(ks),)),
            ],
            input_output_aliases={2 * len(ks) + 2: 0} if extra else {},
        )(hi, out_weights, *pieces, *mixes, *extra)

    def swap(a):
        return lax.ppermute(a, "space", [(0, 1), (1, 0)])

    def route(k):
        pairs = []
        for z in range(high):
            for lo in range(2):
                for s in range(2):
                    there = z ^ k
                    to = (there * 2 + (s ^ (there >= half))) * 2 + (lo ^ (z >= half))
                    pairs.append(((z * 2 + lo) * 2 + s, to))
        return pairs

    def permute(piece, k):
        return lax.ppermute(piece, ("tm", "space"), route(k))

    order = list(range(high - 1, -1, -1))
    heavy, light = order[:half], order[half:]

    def exchange(pieces, ks):
        return {k: permute(pieces[k], k) for k in ks}

    kv, first, weight, gain, *xs = load(after(x, hi))
    others = [swap(kv)]
    q0, q1, kv1 = second(first, xs[1], gain, weight)
    others.append(swap(kv1))
    queries, keys = [q0, q1], [kv, kv1]
    pieces, arrived, home = [], [], []
    last = q1
    for c in range(CHUNKS):
        made, got = {}, {}
        for name, ks in (("far", heavy), ("near", light)):
            q = after(queries[c], last)
            outs = height(ks, xs[c], q, keys[c], others[c])
            last = outs[0]
            made.update(zip(ks, outs))
            ready = dict(made)
            if c and name == "far":
                ready[heavy[-1]] = after(made[heavy[-1]], arrived[-1][heavy[-1]])
            got.update(exchange(ready, ks))
        pieces.append(made)
        arrived.append(got)
    mixes = None
    for c in range(CHUNKS):
        got = [arrived[c][k] for k in range(high)]
        q, kv = time_project(after(got, last))
        other = swap(kv)
        if mixes is not None:
            mixes = after(mixes, q)
            home[-1].update(exchange(mixes, light))
        mixes = timed(q, kv, other)
        last = mixes[0]
        home.append(exchange(mixes, heavy))
        if c + 1 < CHUNKS:
            hi = gate(after(hi, last))
            last = hi
    home[-1].update(exchange(mixes, light))
    out = None
    for c in range(CHUNKS):
        for ks in (light, heavy):
            made = after([pieces[c][k] for k in ks], last)
            mixes = [home[c][k] for k in ks]
            out = finish(c, ks, hi, made, mixes, out)
    return out[None]


def attend_plain(stream, gain, qkv_weight, out_weight):
    groups, length, _ = stream.shape
    inner = out_weight.shape[0]
    heads = inner // HEAD
    wide = stream.astype(jnp.float32)
    normed = normalise(wide, gain)
    projected = jnp.einsum(
        "glf,fe->gle", normed, qkv_weight, preferred_element_type=jnp.float32
    ).astype(jnp.bfloat16)
    q, k, v = jnp.split(projected.reshape(groups, length, 3 * heads, HEAD), 3, axis=2)
    scores = jnp.einsum("gqhd,gkhd->ghqk", q, k, preferred_element_type=jnp.float32) * HEAD**-0.5
    weights = jax.nn.softmax(scores, axis=-1).astype(jnp.bfloat16)
    mixture = jnp.einsum("ghqk,gkhd->gqhd", weights, v, preferred_element_type=jnp.float32)
    mixture = mixture.astype(jnp.bfloat16).reshape(groups, length, inner)
    update = jnp.einsum("gle,ef->glf", mixture, out_weight, preferred_element_type=jnp.float32)
    return (wide + update).astype(jnp.bfloat16)


def plain(tokens, gains, qkv_weights, out_weights):
    frames = lax.axis_size("tm")
    local = lax.all_to_all(tokens[0], "space", split_axis=1, concat_axis=0, tiled=True)
    height_n, wide, feat = local.shape
    by_column = jnp.transpose(local, (1, 0, 2))
    done = attend_plain(by_column, gains[0], qkv_weights[0], out_weights[0])
    flat = done.reshape(frames, wide * height_n // frames, feat)
    by_frame = lax.all_to_all(flat, "tm", split_axis=0, concat_axis=0, tiled=True)
    done = attend_plain(
        jnp.transpose(by_frame, (1, 0, 2)), gains[1], qkv_weights[1], out_weights[1]
    )
    back = lax.all_to_all(
        jnp.transpose(done, (1, 0, 2)), "tm", split_axis=0, concat_axis=0, tiled=True
    )
    by_row = jnp.transpose(back.reshape(wide, height_n, feat), (1, 0, 2))
    return lax.all_to_all(by_row, "space", split_axis=0, concat_axis=1, tiled=True)[None]


def solution(mesh):
    frames, pair = mesh.shape["tm"], mesh.shape["space"]
    high = frames // 2

    def shards(tokens, gains, qkv_weights, out_weights):
        _, rows, cols, feat = tokens.shape
        inner = out_weights.shape[1]
        count = rows * cols // CHUNKS
        fits = (
            pair == 2
            and frames == 2 * high
            and high > 1
            and high & (high - 1) == 0
            and cols == CHUNKS * COLB * high
            and count % (high * POSB) == 0
            and inner % (QUAD * HEAD) == 0
            and feat % 128 == 0
        )
        body = fast if fits else plain
        return body(tokens, gains, qkv_weights, out_weights)

    return jax.shard_map(
        shards,
        mesh=mesh,
        in_specs=(P(("grp", "tm"), "space", None, None), P(), P(), P()),
        out_specs=P(("grp", "tm"), "space", None, None),
        check_vma=False,
    )
```

```python
import functools

import jax
import jax.numpy as jnp
from jax import lax
from jax.experimental import pallas as pl
from jax.experimental.pallas import tpu as pltpu
from jax.sharding import PartitionSpec as P


HEAD = 64
EPS = 1e-06
QUAD = 4
CHUNKS = 2
COLB = 8
SPLIT = 4
POSB = 16
NEG = -1e30
VMEM_BYTES = 16 * 1024 * 1024


def params():
    return pltpu.CompilerParams(vmem_limit_bytes=VMEM_BYTES)


def normalise(stream, gain):
    scale = lax.rsqrt(jnp.mean(stream * stream, axis=-1, keepdims=True) + EPS)
    return (stream * scale * gain).astype(jnp.bfloat16)


def group_bias(keys, group):
    left = lax.broadcasted_iota(jnp.int32, (1, group, keys), 1)
    right = lax.broadcasted_iota(jnp.int32, (1, group, keys), 2) % group
    return jnp.where(left == right, 0.0, NEG)


def attend_quad(query, key, value, bias):
    rows, width = query.shape
    keys = key.shape[0]
    lanes = lax.broadcasted_iota(jnp.int32, (rows, width), 1) // HEAD
    heads = width // HEAD
    zero = jnp.zeros_like(query)
    stacked = jnp.concatenate([jnp.where(lanes == h, query, zero) for h in range(heads)], axis=0)
    scores = lax.dot_general(
        stacked, key, (((1,), (1,)), ((), ())), preferred_element_type=jnp.float32
    )
    scores = scores.reshape(heads * rows // bias.shape[1], bias.shape[1], keys) + bias
    raised = jnp.exp(scores - jnp.max(scores, axis=-1, keepdims=True))
    total = jnp.sum(raised, axis=-1, keepdims=True).reshape(heads * rows, 1)
    raised = raised.reshape(heads * rows, keys).astype(jnp.bfloat16)
    mixed = jnp.dot(raised, value, preferred_element_type=jnp.float32) * (1.0 / total)
    out = mixed[:rows]
    for h in range(1, heads):
        out = jnp.where(lanes == h, mixed[h * rows : (h + 1) * rows], out)
    return out.astype(jnp.bfloat16)


def attend(q_ref, kv_ref, other_ref, spans, group, put):
    inner = q_ref.shape[1]
    width = QUAD * HEAD
    keys = 2 * sum(size for _, size in spans[0])
    bias = group_bias(keys, group)

    def rows(ref, span, lo):
        return [ref[at : at + size, lo : lo + width] for at, size in span]

    def join(parts):
        return parts[0] if len(parts) == 1 else jnp.concatenate(parts, axis=0)

    for span in spans:
        for lo in range(0, inner, width):
            key = join(rows(kv_ref, span, lo) + rows(other_ref, span, lo))
            value = join(rows(kv_ref, span, inner + lo) + rows(other_ref, span, inner + lo))
            put(span, lo, attend_quad(join(rows(q_ref, span, lo)), key, value, bias))


def project_keys(normed, w_ref, kv_ref):
    inner = kv_ref.shape[1] // 2
    kv_ref[...] = jnp.dot(
        normed, w_ref[:, inner:], preferred_element_type=jnp.float32
    ).astype(jnp.bfloat16)


def project_queries(normed, w_ref, q_ref):
    q_ref[...] = jnp.dot(
        normed, w_ref[:, : q_ref.shape[1]], preferred_element_type=jnp.float32
    ).astype(jnp.bfloat16) * jnp.bfloat16(HEAD**-0.5)


def load_kernel(x_ref, gain_ref, w_ref, kv_ref, normed_ref, w_out, gain_out, *refs):
    x_outs, (x_sem, w_sem, gain_sem) = refs[:CHUNKS], refs[CHUNKS:]
    blocks, rows, colb, feat = x_outs[0].shape
    inner = kv_ref.shape[1] // 2
    loads = [
        pltpu.make_async_copy(
            x_ref.at[:, pl.ds((c * blocks + b) * colb, colb), :],
            x_outs[c].at[b],
            x_sem.at[c * blocks + b],
        )
        for c in range(CHUNKS)
        for b in range(blocks)
    ]
    step = feat // SPLIT
    fetches = [
        pltpu.make_async_copy(
            w_ref.at[0, pl.ds(i * step, step), :], w_out.at[pl.ds(i * step, step), :], w_sem.at[i]
        )
        for i in range(SPLIT)
    ]
    gain_load = pltpu.make_async_copy(gain_ref, gain_out, gain_sem)
    for copy in [gain_load] + loads[:blocks] + fetches + loads[blocks:]:
        copy.start()
    gain_load.wait()
    per = rows * colb
    for b in range(blocks):
        loads[b].wait()
        stream = x_outs[0][b].astype(jnp.float32).reshape(per, feat)
        normed_ref[b * per : (b + 1) * per, :] = normalise(stream, gain_out[0:1, :])
    total = None
    for i, fetch in enumerate(fetches):
        fetch.wait()
        span = slice(i * step, (i + 1) * step)
        part = jnp.dot(
            normed_ref[:, span], w_out[span, inner:], preferred_element_type=jnp.float32
        )
        total = part if total is None else total + part
    kv_ref[...] = total.astype(jnp.bfloat16)
    for load in loads[blocks:]:
        load.wait()


def second_kernel(first_ref, x_ref, gain_ref, w_ref, q0_ref, q_ref, kv_ref):
    blocks, rows, colb, feat = x_ref.shape
    stream = x_ref[...].astype(jnp.float32).reshape(blocks * rows * colb, feat)
    normed = normalise(stream, gain_ref[0:1, :])
    project_keys(normed, w_ref, kv_ref)
    project_queries(first_ref[...], w_ref, q0_ref)
    project_queries(normed, w_ref, q_ref)


def height_kernel(ks, hi_ref, x_ref, q_ref, kv_ref, other_ref, w_ref, *refs):
    mix_ref, w_buf, w_sem = refs[-3:]
    _, rows, colb, feat = x_ref.shape
    per = rows * colb
    fetch = pltpu.make_async_copy(w_ref.at[0], w_buf, w_sem)
    fetch.start()
    inner = q_ref.shape[1]
    width = QUAD * HEAD
    bias = group_bias(2 * per, colb)
    places = [jnp.bitwise_xor(hi_ref[0], k) for k in ks]
    for i, place in enumerate(places):
        span = pl.ds(pl.multiple_of(place * per, per), per)
        for lo in range(0, inner, width):
            here, there = slice(lo, lo + width), slice(inner + lo, inner + lo + width)
            key = jnp.concatenate([kv_ref[span, here], other_ref[span, here]], axis=0)
            value = jnp.concatenate([kv_ref[span, there], other_ref[span, there]], axis=0)
            mix_ref[i * per : (i + 1) * per, here] = attend_quad(
                q_ref[span, here], key, value, bias
            )
    fetch.wait()
    update = jnp.dot(mix_ref[...], w_buf[...], preferred_element_type=jnp.float32)
    for i, place in enumerate(places):
        stream = x_ref[place].astype(jnp.float32).reshape(per, feat)
        refs[i][...] = (stream + update[i * per : (i + 1) * per]).astype(jnp.bfloat16)


def time_project_kernel(*refs):
    gain_ref, w_ref, q_ref, kv_ref = refs[-4:]
    normed = jnp.concatenate(
        [normalise(ref[...].astype(jnp.float32), gain_ref[1:2, :]) for ref in refs[:-4]], axis=0
    )
    project_keys(normed, w_ref, kv_ref)
    project_queries(normed, w_ref, q_ref)


def gate_kernel(in_ref, out_ref):
    out_ref[0] = in_ref[0]


def time_kernel(held, q_ref, kv_ref, other_ref, *refs):
    held_refs, mix_refs = refs[:held], refs[held:]
    each = q_ref.shape[0] // len(mix_refs)
    bases = [0 if ref.shape[0] == each else each for ref in mix_refs]
    spans = [
        [(k * each + p, POSB) for k in range(len(mix_refs))] for p in range(0, each, POSB)
    ]
    for ref, held_ref in zip(mix_refs, held_refs):
        ref[:each, :] = held_ref[...]

    def put(span, lo, out):
        at = span[0][0]
        for k, ref in enumerate(mix_refs):
            row = bases[k] + at
            ref[row : row + POSB, lo : lo + out.shape[1]] = out[k * POSB : (k + 1) * POSB]

    attend(q_ref, kv_ref, other_ref, spans, POSB, put)


def finish_kernel(items, mixed, high, hi_ref, w_ref, *refs):
    pieces, mixes = refs[: len(items)], refs[len(items) : len(items) + mixed]
    out_ref, buf, sem = refs[-3:]
    _, rows, colb, feat = buf.shape
    per = rows * colb
    update = jnp.dot(
        jnp.concatenate([ref[...] for ref in mixes], axis=0),
        w_ref[...],
        preferred_element_type=jnp.float32,
    )
    copies = []
    for i, (c, k) in enumerate(items):
        total = pieces[i][...].astype(jnp.float32) + update[i * per : (i + 1) * per]
        buf[i] = total.reshape(rows, colb, feat).astype(jnp.bfloat16)
        place = c * high + jnp.bitwise_xor(hi_ref[0], k)
        column = pl.multiple_of(place * colb, colb)
        copies.append(
            pltpu.make_async_copy(buf.at[i], out_ref.at[:, pl.ds(column, colb), :], sem.at[i])
        )
        copies[-1].start()
    for copy in copies:
        copy.wait()


SMEM = pl.BlockSpec(memory_space=pltpu.SMEM)
HBM = pl.BlockSpec(memory_space=pltpu.HBM)


def cost(flops, moved):
    return pl.CostEstimate(flops=int(flops), bytes_accessed=int(moved), transcendentals=0)


def fast(tokens, gains, qkv_weights, out_weights):
    high = lax.axis_size("tm") // 2
    half = high // 2
    hi = (lax.axis_index("tm") // 2).astype(jnp.int32)[None]
    rows, cols, feat = tokens.shape[1:]
    inner = out_weights.shape[1]
    wide = cols // CHUNKS
    blocks = wide // COLB
    count = rows * wide
    each = count // high
    bf = jnp.bfloat16
    x = pltpu.with_memory_space_constraint(tokens[0], pltpu.HBM)
    gains_far = pltpu.with_memory_space_constraint(gains, pltpu.HBM)
    qkv_far = pltpu.with_memory_space_constraint(qkv_weights, pltpu.HBM)
    out_far = pltpu.with_memory_space_constraint(out_weights, pltpu.HBM)

    def pick(i, n):
        return pl.BlockSpec((None,) + n, lambda _: (i,) + (0,) * len(n))

    def whole(*shape):
        return pl.BlockSpec(shape, lambda _: (0,) * len(shape))

    def call(kernel, flops, **rest):
        return pl.pallas_call(
            kernel,
            grid=(1,),
            compiler_params=params(),
            cost_estimate=cost(flops, 4 * count * feat),
            **rest,
        )

    qkv_out = dict(
        out_specs=[whole(count, inner), whole(count, 2 * inner)],
        out_shape=[
            jax.ShapeDtypeStruct((count, inner), bf),
            jax.ShapeDtypeStruct((count, 2 * inner), bf),
        ],
    )
    qkv_in = [whole(count, inner), whole(count, 2 * inner), whole(count, 2 * inner)]
    work = 2 * count * feat * inner

    def after(values, earlier):
        return lax.optimization_barrier((values, earlier))[0]

    tile = (blocks, rows, COLB, feat)

    def load(x):
        shapes = [(count, 2 * inner), (count, feat), (feat, 3 * inner), gains.shape]
        shapes += [tile] * CHUNKS
        kinds = [bf, bf, bf, gains.dtype] + [bf] * CHUNKS
        return call(
            load_kernel,
            2 * work,
            in_specs=[HBM, HBM, HBM],
            out_specs=[whole(*shape) for shape in shapes],
            out_shape=[jax.ShapeDtypeStruct(*pair) for pair in zip(shapes, kinds)],
            scratch_shapes=[
                pltpu.SemaphoreType.DMA((blocks * CHUNKS,)),
                pltpu.SemaphoreType.DMA((SPLIT,)),
                pltpu.SemaphoreType.DMA,
            ],
        )(x, gains_far, qkv_far)

    def second(first, x, gain, weight):
        return call(
            second_kernel,
            4 * work,
            in_specs=[
                whole(count, feat),
                whole(*tile),
                whole(*gains.shape),
                whole(feat, 3 * inner),
            ],
            out_specs=[whole(count, inner)] + qkv_out["out_specs"],
            out_shape=[jax.ShapeDtypeStruct((count, inner), bf)] + qkv_out["out_shape"],
        )(first, x, gain, weight)

    def height(ks, x, q, kv, other):
        return call(
            functools.partial(height_kernel, ks),
            2 * work,
            in_specs=[SMEM, whole(*tile)] + qkv_in + [HBM],
            out_specs=[whole(each, feat)] * len(ks),
            out_shape=[jax.ShapeDtypeStruct((each, feat), bf)] * len(ks),
            scratch_shapes=[
                pltpu.VMEM((len(ks) * each, inner), bf),
                pltpu.VMEM((inner, feat), bf),
                pltpu.SemaphoreType.DMA,
            ],
        )(hi, x, q, kv, other, out_far)

    def gate(value):
        return pl.pallas_call(
            gate_kernel,
            in_specs=[SMEM],
            out_specs=SMEM,
            out_shape=jax.ShapeDtypeStruct(value.shape, value.dtype),
            compiler_params=params(),
            cost_estimate=cost(1, 8),
            name="gate",
        )(value)

    def time_project(pieces):
        return call(
            time_project_kernel,
            3 * work,
            in_specs=[whole(each, feat)] * high
            + [whole(*gains.shape), pick(1, (feat, 3 * inner))],
            **qkv_out,
        )(*pieces, gains, qkv_weights)

    def timed(q, kv, other, held):
        sizes = [each * (1 + (k < len(held))) for k in range(high)]
        return call(
            functools.partial(time_kernel, len(held)),
            2 * work,
            in_specs=qkv_in + [whole(each, inner)] * len(held),
            out_specs=[whole(size, inner) for size in sizes],
            out_shape=[jax.ShapeDtypeStruct((size, inner), bf) for size in sizes],
        )(q, kv, other, *held)

    def finish(items, hi, pieces, mixes, prior):
        extra_specs, extra = [], []
        if prior is not None:
            extra_specs, extra = [pl.BlockSpec(memory_space=pl.ANY)], [prior]
        return call(
            functools.partial(finish_kernel, items, len(mixes), high),
            work * len(items) // high,
            in_specs=[SMEM, pick(1, (inner, feat))]
            + [whole(each, feat)] * len(items)
            + [whole(*mix.shape) for mix in mixes]
            + extra_specs,
            out_specs=HBM,
            out_shape=jax.ShapeDtypeStruct((rows, cols, feat), bf),
            scratch_shapes=[
                pltpu.VMEM((len(items), rows, COLB, feat), bf),
                pltpu.SemaphoreType.DMA((len(items),)),
            ],
            input_output_aliases={len(items) + len(mixes) + 2: 0} if extra else {},
        )(hi, out_weights, *pieces, *mixes, *extra)

    def swap(a):
        return lax.ppermute(a, "space", [(0, 1), (1, 0)])

    def route(k):
        pairs = []
        for z in range(high):
            for lo in range(2):
                for s in range(2):
                    there = z ^ k
                    to = (there * 2 + (s ^ (there >= half))) * 2 + (lo ^ (z >= half))
                    pairs.append(((z * 2 + lo) * 2 + s, to))
        return pairs

    def permute(piece, k):
        return lax.ppermute(piece, ("tm", "space"), route(k))

    order = list(range(high - 1, -1, -1))
    heavy, light = order[:half], order[half:]

    def exchange(pieces, ks):
        return {k: permute(pieces[k], k) for k in ks}

    kv, first, weight, gain, *xs = load(after(x, hi))
    others = [swap(kv)]
    q0, q1, kv1 = second(first, xs[1], gain, weight)
    others.append(swap(kv1))
    queries, keys = [q0, q1], [kv, kv1]
    pieces, arrived = [], []
    last = q1
    for c in range(CHUNKS):
        made, got = {}, {}
        for name, ks in (("far", heavy), ("near", light)):
            q = after(queries[c], last)
            outs = height(ks, xs[c], q, keys[c], others[c])
            last = outs[0]
            made.update(zip(ks, outs))
            ready = dict(made)
            if c and name == "far":
                ready[heavy[-1]] = after(made[heavy[-1]], arrived[-1][heavy[-1]])
            got.update(exchange(ready, ks))
        pieces.append(made)
        arrived.append(got)
    held, home = [], []
    for c in range(CHUNKS):
        got = [arrived[c][k] for k in range(high)]
        q, kv = time_project(after(got, last))
        mixes = timed(q, kv, swap(kv), held)
        last = mixes[-1]
        home.append(exchange(mixes, heavy))
        held = mixes[:half]
        if c + 1 < CHUNKS:
            hi = gate(after(hi, last))
            last = hi
    shared = exchange(held, light)

    def close(items, mixes, prior):
        made = after([pieces[c][k] for c, k in items], last)
        return finish(items, hi, made, mixes, prior)

    out = close([(0, k) for k in heavy], [home[0][k] for k in heavy], None)
    items = [(c, k) for k in light for c in range(CHUNKS)]
    out = close(items, [shared[k] for k in light], out)
    out = close([(1, k) for k in heavy], [home[1][k] for k in heavy], out)
    return out[None]


def attend_plain(stream, gain, qkv_weight, out_weight):
    groups, length, _ = stream.shape
    inner = out_weight.shape[0]
    heads = inner // HEAD
    wide = stream.astype(jnp.float32)
    normed = normalise(wide, gain)
    projected = jnp.einsum(
        "glf,fe->gle", normed, qkv_weight, preferred_element_type=jnp.float32
    ).astype(jnp.bfloat16)
    q, k, v = jnp.split(projected.reshape(groups, length, 3 * heads, HEAD), 3, axis=2)
    scores = jnp.einsum("gqhd,gkhd->ghqk", q, k, preferred_element_type=jnp.float32) * HEAD**-0.5
    weights = jax.nn.softmax(scores, axis=-1).astype(jnp.bfloat16)
    mixture = jnp.einsum("ghqk,gkhd->gqhd", weights, v, preferred_element_type=jnp.float32)
    mixture = mixture.astype(jnp.bfloat16).reshape(groups, length, inner)
    update = jnp.einsum("gle,ef->glf", mixture, out_weight, preferred_element_type=jnp.float32)
    return (wide + update).astype(jnp.bfloat16)


def plain(tokens, gains, qkv_weights, out_weights):
    frames = lax.axis_size("tm")
    local = lax.all_to_all(tokens[0], "space", split_axis=1, concat_axis=0, tiled=True)
    height_n, wide, feat = local.shape
    by_column = jnp.transpose(local, (1, 0, 2))
    done = attend_plain(by_column, gains[0], qkv_weights[0], out_weights[0])
    flat = done.reshape(frames, wide * height_n // frames, feat)
    by_frame = lax.all_to_all(flat, "tm", split_axis=0, concat_axis=0, tiled=True)
    done = attend_plain(
        jnp.transpose(by_frame, (1, 0, 2)), gains[1], qkv_weights[1], out_weights[1]
    )
    back = lax.all_to_all(
        jnp.transpose(done, (1, 0, 2)), "tm", split_axis=0, concat_axis=0, tiled=True
    )
    by_row = jnp.transpose(back.reshape(wide, height_n, feat), (1, 0, 2))
    return lax.all_to_all(by_row, "space", split_axis=0, concat_axis=1, tiled=True)[None]


def solution(mesh):
    frames, pair = mesh.shape["tm"], mesh.shape["space"]
    high = frames // 2

    def shards(tokens, gains, qkv_weights, out_weights):
        _, rows, cols, feat = tokens.shape
        inner = out_weights.shape[1]
        count = rows * cols // CHUNKS
        fits = (
            pair == 2
            and frames == 2 * high
            and high > 1
            and high & (high - 1) == 0
            and cols == CHUNKS * COLB * high
            and count % (high * POSB) == 0
            and inner % (QUAD * HEAD) == 0
            and feat % 128 == 0
        )
        body = fast if fits else plain
        return body(tokens, gains, qkv_weights, out_weights)

    return jax.shard_map(
        shards,
        mesh=mesh,
        in_specs=(P(("grp", "tm"), "space", None, None), P(), P(), P()),
        out_specs=P(("grp", "tm"), "space", None, None),
        check_vma=False,
    )
```

```python
import functools

import jax
import jax.numpy as jnp
from jax import lax
from jax.experimental import pallas as pl
from jax.experimental.pallas import tpu as pltpu
from jax.sharding import PartitionSpec as P


HEAD = 64
EPS = 1e-06
QUAD = 4
CHUNKS = 2
COLB = 8
SPLIT = 2
LATE = ()
POSB = 16
NEG = -1e30
VMEM_BYTES = 16 * 1024 * 1024


def params():
    return pltpu.CompilerParams(vmem_limit_bytes=VMEM_BYTES)


def normalise(stream, gain):
    scale = lax.rsqrt(jnp.mean(stream * stream, axis=-1, keepdims=True) + EPS)
    return (stream * scale * gain).astype(jnp.bfloat16)


def group_bias(keys, group):
    left = lax.broadcasted_iota(jnp.int32, (1, group, keys), 1)
    right = lax.broadcasted_iota(jnp.int32, (1, group, keys), 2) % group
    return jnp.where(left == right, 0.0, NEG)


def attend_quad(query, key, value, bias):
    rows, width = query.shape
    keys = key.shape[0]
    lanes = lax.broadcasted_iota(jnp.int32, (rows, width), 1) // HEAD
    heads = width // HEAD
    zero = jnp.zeros_like(query)
    stacked = jnp.concatenate([jnp.where(lanes == h, query, zero) for h in range(heads)], axis=0)
    scores = lax.dot_general(
        stacked, key, (((1,), (1,)), ((), ())), preferred_element_type=jnp.float32
    )
    scores = scores.reshape(heads * rows // bias.shape[1], bias.shape[1], keys) + bias
    raised = jnp.exp(scores - jnp.max(scores, axis=-1, keepdims=True))
    total = jnp.sum(raised, axis=-1, keepdims=True).reshape(heads * rows, 1)
    raised = raised.reshape(heads * rows, keys).astype(jnp.bfloat16)
    mixed = jnp.dot(raised, value, preferred_element_type=jnp.float32) * (1.0 / total)
    out = mixed[:rows]
    for h in range(1, heads):
        out = jnp.where(lanes == h, mixed[h * rows : (h + 1) * rows], out)
    return out.astype(jnp.bfloat16)


def join(parts):
    return parts[0] if len(parts) == 1 else jnp.concatenate(parts, axis=0)


def project_keys(normed, w_ref, kv_ref):
    inner = kv_ref.shape[1] // 2
    kv_ref[...] = jnp.dot(
        normed, w_ref[:, inner:], preferred_element_type=jnp.float32
    ).astype(jnp.bfloat16)


def project_queries(normed, w_ref, q_ref):
    q_ref[...] = jnp.dot(
        normed, w_ref[:, : q_ref.shape[1]], preferred_element_type=jnp.float32
    ).astype(jnp.bfloat16) * jnp.bfloat16(HEAD**-0.5)


def position():
    return lax.axis_index("tm") // 2


def load_kernel(order, x_ref, gain_ref, w_ref, kv_ref, normed_ref, w_out, gain_out, *refs):
    x_outs, (x_sem, w_sem, gain_sem) = refs[:CHUNKS], refs[CHUNKS:]
    blocks, rows, colb, feat = x_outs[0].shape
    inner = kv_ref.shape[1] // 2
    per = rows * colb
    first = kv_ref.shape[0] // per
    loads = []
    for c in range(CHUNKS):
        for i, k in enumerate(order):
            column = pl.multiple_of((c * blocks + jnp.bitwise_xor(position(), k)) * colb, colb)
            loads.append(
                pltpu.make_async_copy(
                    x_ref.at[:, pl.ds(column, colb), :], x_outs[c].at[i], x_sem.at[c * blocks + i]
                )
            )
    step = feat // SPLIT
    fetches = [
        pltpu.make_async_copy(
            w_ref.at[0, pl.ds(i * step, step), :], w_out.at[pl.ds(i * step, step), :], w_sem.at[i]
        )
        for i in range(SPLIT)
    ]
    gain_load = pltpu.make_async_copy(gain_ref, gain_out, gain_sem)
    for copy in [gain_load] + loads[:first] + fetches + loads[first:]:
        copy.start()
    gain_load.wait()
    for i in range(first):
        loads[i].wait()
        stream = x_outs[0][i].astype(jnp.float32).reshape(per, feat)
        normed_ref[i * per : (i + 1) * per, :] = normalise(stream, gain_out[0:1, :])
    total = None
    for i, fetch in enumerate(fetches):
        fetch.wait()
        span = slice(i * step, (i + 1) * step)
        part = jnp.dot(
            normed_ref[:, span], w_out[span, inner:], preferred_element_type=jnp.float32
        )
        total = part if total is None else total + part
    kv_ref[...] = total.astype(jnp.bfloat16)
    for load in loads[first:]:
        load.wait()


def queries_kernel(normed_ref, w_ref, q_ref):
    project_queries(normed_ref[...], w_ref, q_ref)


def project_kernel(first, x_ref, gain_ref, w_ref, q_ref, kv_ref):
    blocks, rows, colb, feat = x_ref.shape
    stream = x_ref[first:].astype(jnp.float32).reshape((blocks - first) * rows * colb, feat)
    normed = normalise(stream, gain_ref[0:1, :])
    project_keys(normed, w_ref, kv_ref)
    project_queries(normed, w_ref, q_ref)


def height_kernel(tile, start, x_ref, q_ref, kv_ref, other_ref, w_ref, *refs):
    mix_ref, w_buf, w_sem = refs[-3:]
    _, rows, colb, feat = x_ref.shape
    per = rows * colb
    fetch = pltpu.make_async_copy(w_ref.at[0], w_buf, w_sem)
    fetch.start()
    inner = q_ref.shape[1]
    width = QUAD * HEAD
    bias = group_bias(2 * per, colb)
    zero = lax.axis_index("space") // lax.axis_size("space")
    for i in range(len(refs) - 3):
        span = pl.ds(pl.multiple_of((zero + i) * per, per) + start, per)
        for lo in range(0, inner, width):
            here, there = slice(lo, lo + width), slice(inner + lo, inner + lo + width)
            key = join([kv_ref[span, here], other_ref[span, here]])
            value = join([kv_ref[span, there], other_ref[span, there]])
            mix_ref[i * per : (i + 1) * per, here] = attend_quad(
                q_ref[span, here], key, value, bias
            )
    fetch.wait()
    update = jnp.dot(mix_ref[...], w_buf[...], preferred_element_type=jnp.float32)
    for i in range(len(refs) - 3):
        stream = x_ref[tile + i].astype(jnp.float32).reshape(per, feat)
        refs[i][...] = (stream + update[i * per : (i + 1) * per]).astype(jnp.bfloat16)


def time_project_kernel(*refs):
    gain_ref, w_ref, q_ref, kv_ref = refs[-4:]
    normed = join([normalise(ref[...].astype(jnp.float32), gain_ref[1:2, :]) for ref in refs[:-4]])
    project_keys(normed, w_ref, kv_ref)
    project_queries(normed, w_ref, q_ref)


def gate_kernel(in_ref, out_ref):
    out_ref[0] = 0


def time_kernel(groups, *refs):
    count = 3 * len(groups)
    sources, mix_refs = refs[:count], refs[count:]
    each, inner = mix_refs[0].shape
    width = QUAD * HEAD
    bias = group_bias(2 * len(mix_refs) * POSB, POSB)
    flat = [(g, i, k) for g, group in enumerate(groups) for i, k in enumerate(group)]

    def rows(which, p, lo):
        return [
            sources[3 * g + which][i * each + p : i * each + p + POSB, lo : lo + width]
            for g, i, _ in flat
        ]

    for p in range(0, each, POSB):
        for lo in range(0, inner, width):
            key = join(rows(1, p, lo) + rows(2, p, lo))
            value = join(rows(1, p, inner + lo) + rows(2, p, inner + lo))
            out = attend_quad(join(rows(0, p, lo)), key, value, bias)
            for n, (_, _, k) in enumerate(flat):
                mix_refs[k][p : p + POSB, lo : lo + width] = out[n * POSB : (n + 1) * POSB]


def finish_kernel(items, mixed, high, w_ref, *refs):
    pieces, mixes = refs[: len(items)], refs[len(items) : len(items) + mixed]
    out_ref, buf, sem = refs[-3:]
    _, rows, colb, feat = buf.shape
    per = rows * colb
    update = jnp.dot(
        jnp.concatenate([ref[...] for ref in mixes], axis=0),
        w_ref[...],
        preferred_element_type=jnp.float32,
    )
    copies = []
    for i, (c, k) in enumerate(items):
        total = pieces[i][...].astype(jnp.float32) + update[i * per : (i + 1) * per]
        buf[i] = total.reshape(rows, colb, feat).astype(jnp.bfloat16)
        place = c * high + jnp.bitwise_xor(position(), k)
        column = pl.multiple_of(place * colb, colb)
        copies.append(
            pltpu.make_async_copy(buf.at[i], out_ref.at[:, pl.ds(column, colb), :], sem.at[i])
        )
        copies[-1].start()
    for copy in copies:
        copy.wait()


SMEM = pl.BlockSpec(memory_space=pltpu.SMEM)
HBM = pl.BlockSpec(memory_space=pltpu.HBM)


def cost(flops, moved):
    return pl.CostEstimate(flops=int(flops), bytes_accessed=int(moved), transcendentals=0)


def fast(tokens, gains, qkv_weights, out_weights):
    high = lax.axis_size("tm") // 2
    half = high // 2
    order = list(range(high - 1, -1, -1))
    rows, cols, feat = tokens.shape[1:]
    inner = out_weights.shape[1]
    wide = cols // CHUNKS
    blocks = wide // COLB
    count = rows * wide
    each = count // high
    bf = jnp.bfloat16
    x = pltpu.with_memory_space_constraint(tokens[0], pltpu.HBM)
    gains_far = pltpu.with_memory_space_constraint(gains, pltpu.HBM)
    qkv_far = pltpu.with_memory_space_constraint(qkv_weights, pltpu.HBM)
    out_far = pltpu.with_memory_space_constraint(out_weights, pltpu.HBM)

    def pick(i, n):
        return pl.BlockSpec((None,) + n, lambda _: (i,) + (0,) * len(n))

    def whole(*shape):
        return pl.BlockSpec(shape, lambda _: (0,) * len(shape))

    def call(kernel, flops, **rest):
        return pl.pallas_call(
            kernel,
            grid=(1,),
            compiler_params=params(),
            cost_estimate=cost(flops, 4 * count * feat),
            **rest,
        )

    tile = (blocks, rows, COLB, feat)
    work = 2 * count * feat * inner // high

    def made(n, width):
        return jax.ShapeDtypeStruct((n * each, width), bf)

    def full(array):
        return whole(*array.shape)

    def load(x):
        shapes = [(half * each, 2 * inner), (half * each, feat), (feat, 3 * inner), gains.shape]
        shapes += [tile] * CHUNKS
        kinds = [bf, bf, bf, gains.dtype] + [bf] * CHUNKS
        return call(
            functools.partial(load_kernel, order),
            2 * half * work,
            in_specs=[HBM, HBM, HBM],
            out_specs=[whole(*shape) for shape in shapes],
            out_shape=[jax.ShapeDtypeStruct(*pair) for pair in zip(shapes, kinds)],
            scratch_shapes=[
                pltpu.SemaphoreType.DMA((blocks * CHUNKS,)),
                pltpu.SemaphoreType.DMA((SPLIT,)),
                pltpu.SemaphoreType.DMA,
            ],
        )(x, gains_far, qkv_far)

    def ask(normed, weight):
        out = made(half, inner)
        return call(
            queries_kernel,
            half * work,
            in_specs=[full(normed), full(weight)],
            out_specs=full(out),
            out_shape=out,
        )(normed, weight)

    def project(first, x, gain, weight):
        outs = [made(high - first, inner), made(high - first, 2 * inner)]
        return call(
            functools.partial(project_kernel, first),
            3 * (high - first) * work,
            in_specs=[full(x), full(gain), full(weight)],
            out_specs=[full(out) for out in outs],
            out_shape=outs,
        )(x, gain, weight)

    def height(at, start, x, q, kv, other):
        outs = [made(1, feat)] * half
        return call(
            functools.partial(height_kernel, at, start),
            2 * half * work,
            in_specs=[full(x), full(q), full(kv), full(other), HBM],
            out_specs=[full(out) for out in outs],
            out_shape=outs,
            scratch_shapes=[
                pltpu.VMEM((half * each, inner), bf),
                pltpu.VMEM((inner, feat), bf),
                pltpu.SemaphoreType.DMA,
            ],
        )(x, q, kv, other, out_far)

    def gate(value):
        return pl.pallas_call(
            gate_kernel,
            in_specs=[pl.BlockSpec(memory_space=pl.ANY)],
            out_specs=SMEM,
            out_shape=jax.ShapeDtypeStruct((1,), jnp.int32),
            compiler_params=params(),
            cost_estimate=cost(1, 8),
            name="gate",
        )(value)

    def time_project(pieces):
        n = len(pieces)
        outs = [made(n, inner), made(n, 2 * inner)]
        return call(
            time_project_kernel,
            3 * n * work,
            in_specs=[full(piece) for piece in pieces]
            + [full(gains), pick(1, (feat, 3 * inner))],
            out_specs=[full(out) for out in outs],
            out_shape=outs,
        )(*pieces, gains, qkv_weights)

    def timed(groups, *sources):
        outs = [made(1, inner)] * high
        return call(
            functools.partial(time_kernel, groups),
            2 * high * work,
            in_specs=[full(source) for source in sources],
            out_specs=[full(out) for out in outs],
            out_shape=outs,
        )(*sources)

    def finish(items, pieces, mixes, extra):
        return call(
            functools.partial(finish_kernel, items, len(mixes), high),
            work * len(items),
            in_specs=[pick(1, (inner, feat))]
            + [whole(each, feat)] * len(items)
            + [whole(*mix.shape) for mix in mixes]
            + [pl.BlockSpec(memory_space=pl.ANY)] * len(extra),
            out_specs=HBM,
            out_shape=jax.ShapeDtypeStruct((rows, cols, feat), bf),
            scratch_shapes=[
                pltpu.VMEM((len(items), rows, COLB, feat), bf),
                pltpu.SemaphoreType.DMA((len(items),)),
            ],
            input_output_aliases={
                1 + len(items) + len(mixes): 0 for a in extra if a.ndim == 3
            },
        )(out_weights, *pieces, *mixes, *extra)

    def after(values, earlier):
        return lax.optimization_barrier((values, earlier))[0]

    def swap(a):
        return lax.ppermute(a, "space", [(0, 1), (1, 0)])

    def route(k):
        pairs = []
        for z in range(high):
            for lo in range(2):
                for s in range(2):
                    there = z ^ k
                    to = (there * 2 + (s ^ (there >= half))) * 2 + (lo ^ (z >= half))
                    pairs.append(((z * 2 + lo) * 2 + s, to))
        return pairs

    def permute(piece, k):
        return lax.ppermute(piece, ("tm", "space"), route(k))

    def exchange(pieces, ks):
        return {k: permute(pieces[k], k) for k in ks}

    heavy, light = order[:half], order[half:]
    kv, normed, weight, gain, *xs = load(x)
    other = swap(kv)
    q = ask(normed, weight)
    outs = height(0, 0, xs[0], q, kv, other)
    pieces = [dict(zip(heavy, outs)), {}]
    arrived = [exchange(pieces[0], heavy), {}]
    q, kv = project(half, after(xs[0], outs[0]), gain, weight)
    other = swap(kv)
    q1, kv1 = project(0, after(xs[1], q), gain, weight)
    other1 = swap(kv1)
    outs = height(half, 0, xs[0], after(q, q1), kv, other)
    pieces[0].update(zip(light, outs))
    arrived[0].update(exchange(pieces[0], light))
    for name, ks, n in (("far", heavy, 0), ("near", light, half)):
        q1 = after(q1, outs[0])
        outs = height(n, n * each, xs[1], q1, kv1, other1)
        pieces[1].update(zip(ks, outs))
        ready = dict(pieces[1])
        if name == "far":
            ready[half] = after(ready[half], arrived[0][half])
        arrived[1].update(exchange(ready, ks))
    last = outs[0]
    plans = [[order], [[k for k in order if k != half], [half]]]
    home, gates = [], []
    for c in range(CHUNKS):
        sources = []
        for n, group in enumerate(plans[c]):
            got = after([arrived[c][k] for k in group], last)
            q, kv = time_project(got)
            sources += [q, kv, swap(kv)]
            last = q
            if c and not n and LATE:
                home[-1].update(exchange(after(mixes, q), LATE))
        mixes = timed(plans[c], *sources)
        last = mixes[0]
        home.append(exchange(mixes, [k for k in order if c or k not in LATE]))
        if c + 1 < CHUNKS:
            last = gate(last)
            gates.append(last)
    out = gates
    for c in range(CHUNKS):
        items = [(c, k) for k in order]
        held = after([pieces[c][k] for k in order], last)
        out = [finish(items, held, [home[c][k] for k in order], out)]
    return out[0][None]


def attend_plain(stream, gain, qkv_weight, out_weight):
    groups, length, _ = stream.shape
    inner = out_weight.shape[0]
    heads = inner // HEAD
    wide = stream.astype(jnp.float32)
    normed = normalise(wide, gain)
    projected = jnp.einsum(
        "glf,fe->gle", normed, qkv_weight, preferred_element_type=jnp.float32
    ).astype(jnp.bfloat16)
    q, k, v = jnp.split(projected.reshape(groups, length, 3 * heads, HEAD), 3, axis=2)
    scores = jnp.einsum("gqhd,gkhd->ghqk", q, k, preferred_element_type=jnp.float32) * HEAD**-0.5
    weights = jax.nn.softmax(scores, axis=-1).astype(jnp.bfloat16)
    mixture = jnp.einsum("ghqk,gkhd->gqhd", weights, v, preferred_element_type=jnp.float32)
    mixture = mixture.astype(jnp.bfloat16).reshape(groups, length, inner)
    update = jnp.einsum("gle,ef->glf", mixture, out_weight, preferred_element_type=jnp.float32)
    return (wide + update).astype(jnp.bfloat16)


def plain(tokens, gains, qkv_weights, out_weights):
    frames = lax.axis_size("tm")
    local = lax.all_to_all(tokens[0], "space", split_axis=1, concat_axis=0, tiled=True)
    height_n, wide, feat = local.shape
    by_column = jnp.transpose(local, (1, 0, 2))
    done = attend_plain(by_column, gains[0], qkv_weights[0], out_weights[0])
    flat = done.reshape(frames, wide * height_n // frames, feat)
    by_frame = lax.all_to_all(flat, "tm", split_axis=0, concat_axis=0, tiled=True)
    done = attend_plain(
        jnp.transpose(by_frame, (1, 0, 2)), gains[1], qkv_weights[1], out_weights[1]
    )
    back = lax.all_to_all(
        jnp.transpose(done, (1, 0, 2)), "tm", split_axis=0, concat_axis=0, tiled=True
    )
    by_row = jnp.transpose(back.reshape(wide, height_n, feat), (1, 0, 2))
    return lax.all_to_all(by_row, "space", split_axis=0, concat_axis=1, tiled=True)[None]


def solution(mesh):
    frames, pair = mesh.shape["tm"], mesh.shape["space"]
    high = frames // 2

    def shards(tokens, gains, qkv_weights, out_weights):
        _, rows, cols, feat = tokens.shape
        inner = out_weights.shape[1]
        count = rows * cols // CHUNKS
        fits = (
            pair == 2
            and frames == 2 * high
            and high > 1
            and high & (high - 1) == 0
            and cols == CHUNKS * COLB * high
            and count % (high * POSB) == 0
            and inner % (QUAD * HEAD) == 0
            and feat % 128 == 0
        )
        body = fast if fits else plain
        return body(tokens, gains, qkv_weights, out_weights)

    return jax.shard_map(
        shards,
        mesh=mesh,
        in_specs=(P(("grp", "tm"), "space", None, None), P(), P(), P()),
        out_specs=P(("grp", "tm"), "space", None, None),
        check_vma=False,
    )
```

```python
import functools

import jax
import jax.numpy as jnp
from jax import lax
from jax.experimental import pallas as pl
from jax.experimental.pallas import tpu as pltpu
from jax.sharding import PartitionSpec as P


HEAD = 64
EPS = 1e-06
QUAD = 4
CHUNKS = 2
COLB = 8
SPLIT = 2
POSB = 16
NEG = -1e30
VMEM_BYTES = 16 * 1024 * 1024


def params():
    return pltpu.CompilerParams(vmem_limit_bytes=VMEM_BYTES)


def normalise(stream, gain):
    scale = lax.rsqrt(jnp.mean(stream * stream, axis=-1, keepdims=True) + EPS)
    return (stream * scale * gain).astype(jnp.bfloat16)


def group_bias(keys, group):
    left = lax.broadcasted_iota(jnp.int32, (1, group, keys), 1)
    right = lax.broadcasted_iota(jnp.int32, (1, group, keys), 2) % group
    return jnp.where(left == right, 0.0, NEG)


def attend_quad(query, key, value, bias):
    rows, width = query.shape
    keys = key.shape[0]
    lanes = lax.broadcasted_iota(jnp.int32, (rows, width), 1) // HEAD
    heads = width // HEAD
    zero = jnp.zeros_like(query)
    stacked = jnp.concatenate([jnp.where(lanes == h, query, zero) for h in range(heads)], axis=0)
    scores = lax.dot_general(
        stacked, key, (((1,), (1,)), ((), ())), preferred_element_type=jnp.float32
    )
    scores = scores.reshape(heads * rows // bias.shape[1], bias.shape[1], keys) + bias
    raised = jnp.exp(scores - jnp.max(scores, axis=-1, keepdims=True))
    total = jnp.sum(raised, axis=-1, keepdims=True).reshape(heads * rows, 1)
    raised = raised.reshape(heads * rows, keys).astype(jnp.bfloat16)
    mixed = jnp.dot(raised, value, preferred_element_type=jnp.float32) * (1.0 / total)
    out = mixed[:rows]
    for h in range(1, heads):
        out = jnp.where(lanes == h, mixed[h * rows : (h + 1) * rows], out)
    return out.astype(jnp.bfloat16)


def join(parts):
    return parts[0] if len(parts) == 1 else jnp.concatenate(parts, axis=0)


def project_keys(normed, weight, kv_ref):
    kv_ref[...] = jnp.dot(normed, weight, preferred_element_type=jnp.float32).astype(jnp.bfloat16)


def project_queries(normed, weight, q_ref):
    q_ref[...] = jnp.dot(normed, weight, preferred_element_type=jnp.float32).astype(
        jnp.bfloat16
    ) * jnp.bfloat16(HEAD**-0.5)


def position():
    return lax.axis_index("tm") // 2


def token_loads(c, ks, high, x_ref, x_out, sem):
    colb = x_out.shape[2]
    loads = []
    for i, k in enumerate(ks):
        column = pl.multiple_of((c * high + jnp.bitwise_xor(position(), k)) * colb, colb)
        loads.append(
            pltpu.make_async_copy(x_ref.at[:, pl.ds(column, colb), :], x_out.at[i], sem.at[i])
        )
    return loads


def load_kernel(ks, high, x_ref, gain_ref, w_ref, kv_ref, normed_ref, w_out, gain_out, *refs):
    x_out, x_sem, w_sem, gain_sem = refs
    _, rows, colb, feat = x_out.shape
    width = kv_ref.shape[1]
    per = rows * colb
    loads = token_loads(0, ks, high, x_ref, x_out, x_sem)
    step = feat // SPLIT
    fetches = [
        pltpu.make_async_copy(
            w_ref.at[0, pl.ds(i * step, step), pl.ds(width // 2, width)],
            w_out.at[pl.ds(i * step, step), :],
            w_sem.at[i],
        )
        for i in range(SPLIT)
    ]
    gain_load = pltpu.make_async_copy(gain_ref, gain_out, gain_sem)
    for copy in [gain_load] + loads + fetches:
        copy.start()
    gain_load.wait()
    for i, load in enumerate(loads):
        load.wait()
        stream = x_out[i].astype(jnp.float32).reshape(per, feat)
        normed_ref[i * per : (i + 1) * per, :] = normalise(stream, gain_out[0:1, :])
    total = None
    for i, fetch in enumerate(fetches):
        fetch.wait()
        span = slice(i * step, (i + 1) * step)
        part = jnp.dot(normed_ref[:, span], w_out[span, :], preferred_element_type=jnp.float32)
        total = part if total is None else total + part
    kv_ref[...] = total.astype(jnp.bfloat16)


def ask_kernel(normed_ref, w_ref, q_ref, w_out, sem):
    fetch = pltpu.make_async_copy(w_ref.at[0, :, pl.ds(0, q_ref.shape[1])], w_out, sem)
    fetch.start()
    fetch.wait()
    project_queries(normed_ref[...], w_out[...], q_ref)


def project_kernel(c, ks, high, x_ref, gain_ref, keys_ref, queries_ref, q_ref, kv_ref, x_out, sem):
    count, rows, colb, feat = x_out.shape
    loads = token_loads(c, ks, high, x_ref, x_out, sem)
    for load in loads:
        load.start()
    for load in loads:
        load.wait()
    stream = x_out[...].astype(jnp.float32).reshape(count * rows * colb, feat)
    normed = normalise(stream, gain_ref[0:1, :])
    project_keys(normed, keys_ref[...], kv_ref)
    project_queries(normed, queries_ref[...], q_ref)


def height_kernel(tile, start, x_ref, q_ref, kv_ref, other_ref, w_ref, *refs):
    mix_ref, w_buf, w_sem = refs[-3:]
    _, rows, colb, feat = x_ref.shape
    per = rows * colb
    fetch = pltpu.make_async_copy(w_ref.at[0], w_buf, w_sem)
    fetch.start()
    inner = q_ref.shape[1]
    width = QUAD * HEAD
    bias = group_bias(2 * per, colb)
    zero = lax.axis_index("space") // lax.axis_size("space")
    for i in range(len(refs) - 3):
        span = pl.ds(pl.multiple_of((zero + i) * per, per) + start, per)
        for lo in range(0, inner, width):
            here, there = slice(lo, lo + width), slice(inner + lo, inner + lo + width)
            key = join([kv_ref[span, here], other_ref[span, here]])
            value = join([kv_ref[span, there], other_ref[span, there]])
            mix_ref[i * per : (i + 1) * per, here] = attend_quad(
                q_ref[span, here], key, value, bias
            )
    fetch.wait()
    update = jnp.dot(mix_ref[...], w_buf[...], preferred_element_type=jnp.float32)
    for i in range(len(refs) - 3):
        stream = x_ref[tile + i].astype(jnp.float32).reshape(per, feat)
        refs[i][...] = (stream + update[i * per : (i + 1) * per]).astype(jnp.bfloat16)


def time_project_kernel(*refs):
    gain_ref, w_ref, q_ref, kv_ref = refs[-4:]
    normed = join([normalise(ref[...].astype(jnp.float32), gain_ref[1:2, :]) for ref in refs[:-4]])
    inner = q_ref.shape[1]
    project_keys(normed, w_ref[:, inner:], kv_ref)
    project_queries(normed, w_ref[:, :inner], q_ref)


def gate_kernel(in_ref, out_ref):
    out_ref[0] = 0


def time_kernel(groups, ks, *refs):
    count = 3 * len(groups)
    sources, mix_refs = refs[:count], refs[count:]
    each, inner = mix_refs[0].shape
    width = QUAD * HEAD
    flat = [(g, i, k) for g, group in enumerate(groups) for i, k in enumerate(group)]

    bias = group_bias(2 * len(flat) * POSB, POSB)

    def rows(which, p, lo, chosen=flat):
        return [
            sources[3 * g + which][i * each + p : i * each + p + POSB, lo : lo + width]
            for g, i, _ in chosen
        ]

    for p in range(0, each, POSB):
        for lo in range(0, inner, width):
            key = join(rows(1, p, lo) + rows(2, p, lo))
            value = join(rows(1, p, inner + lo) + rows(2, p, inner + lo))
            asking = [entry for k in ks for entry in flat if entry[2] == k]
            out = attend_quad(join(rows(0, p, lo, asking)), key, value, bias)
            for n, ref in enumerate(mix_refs):
                ref[p : p + POSB, lo : lo + width] = out[n * POSB : (n + 1) * POSB]


def finish_kernel(items, mixed, high, w_ref, *refs):
    pieces, mixes = refs[: len(items)], refs[len(items) : len(items) + mixed]
    out_ref, buf, sem = refs[-3:]
    _, rows, colb, feat = buf.shape
    per = rows * colb
    update = jnp.dot(
        jnp.concatenate([ref[...] for ref in mixes], axis=0),
        w_ref[...],
        preferred_element_type=jnp.float32,
    )
    copies = []
    for i, (c, k) in enumerate(items):
        total = pieces[i][...].astype(jnp.float32) + update[i * per : (i + 1) * per]
        buf[i] = total.reshape(rows, colb, feat).astype(jnp.bfloat16)
        place = c * high + jnp.bitwise_xor(position(), k)
        column = pl.multiple_of(place * colb, colb)
        copies.append(
            pltpu.make_async_copy(buf.at[i], out_ref.at[:, pl.ds(column, colb), :], sem.at[i])
        )
        copies[-1].start()
    for copy in copies:
        copy.wait()


SMEM = pl.BlockSpec(memory_space=pltpu.SMEM)
HBM = pl.BlockSpec(memory_space=pltpu.HBM)


def cost(flops, moved):
    return pl.CostEstimate(flops=int(flops), bytes_accessed=int(moved), transcendentals=0)


def fast(tokens, gains, qkv_weights, out_weights):
    high = lax.axis_size("tm") // 2
    half = high // 2
    order = list(range(high - 1, -1, -1))
    heavy, light = order[:half], order[half:]
    rows, cols, feat = tokens.shape[1:]
    inner = out_weights.shape[1]
    wide = cols // CHUNKS
    count = rows * wide
    each = count // high
    bf = jnp.bfloat16
    x = pltpu.with_memory_space_constraint(tokens[0], pltpu.HBM)
    gains_far = pltpu.with_memory_space_constraint(gains, pltpu.HBM)
    qkv_far = pltpu.with_memory_space_constraint(qkv_weights, pltpu.HBM)
    out_far = pltpu.with_memory_space_constraint(out_weights, pltpu.HBM)

    def pick(i, n):
        return pl.BlockSpec((None,) + n, lambda _: (i,) + (0,) * len(n))

    def whole(*shape):
        return pl.BlockSpec(shape, lambda _: (0,) * len(shape))

    def call(kernel, flops, **rest):
        return pl.pallas_call(
            kernel,
            grid=(1,),
            compiler_params=params(),
            cost_estimate=cost(flops, 4 * count * feat),
            **rest,
        )

    work = 2 * count * feat * inner // high

    def made(n, width):
        return jax.ShapeDtypeStruct((n * each, width), bf)

    def full(array):
        return whole(*array.shape)

    def tiles(n):
        return jax.ShapeDtypeStruct((n, rows, COLB, feat), bf)

    def load(x):
        outs = [
            made(half, 2 * inner),
            made(half, feat),
            jax.ShapeDtypeStruct((feat, 2 * inner), bf),
            jax.ShapeDtypeStruct(gains.shape, gains.dtype),
            tiles(half),
        ]
        return call(
            functools.partial(load_kernel, heavy, high),
            2 * half * work,
            in_specs=[HBM, HBM, HBM],
            out_specs=[full(out) for out in outs],
            out_shape=outs,
            scratch_shapes=[
                pltpu.SemaphoreType.DMA((half,)),
                pltpu.SemaphoreType.DMA((SPLIT,)),
                pltpu.SemaphoreType.DMA,
            ],
        )(x, gains_far, qkv_far)

    def ask(normed):
        outs = [made(half, inner), jax.ShapeDtypeStruct((feat, inner), bf)]
        return call(
            ask_kernel,
            half * work,
            in_specs=[full(normed), HBM],
            out_specs=[full(out) for out in outs],
            out_shape=outs,
            scratch_shapes=[pltpu.SemaphoreType.DMA],
        )(normed, qkv_far)

    def project(c, ks, x, gain, keys, queries):
        n = len(ks)
        outs = [made(n, inner), made(n, 2 * inner), tiles(n)]
        return call(
            functools.partial(project_kernel, c, ks, high),
            3 * n * work,
            in_specs=[HBM, full(gain), full(keys), full(queries)],
            out_specs=[full(out) for out in outs],
            out_shape=outs,
            scratch_shapes=[pltpu.SemaphoreType.DMA((n,))],
        )(x, gain, keys, queries)

    def height(n, at, x, q, kv, other):
        outs = [made(1, feat)] * n
        return call(
            functools.partial(height_kernel, at, at * each),
            2 * n * work,
            in_specs=[full(x), full(q), full(kv), full(other), HBM],
            out_specs=[full(out) for out in outs],
            out_shape=outs,
            scratch_shapes=[
                pltpu.VMEM((n * each, inner), bf),
                pltpu.VMEM((inner, feat), bf),
                pltpu.SemaphoreType.DMA,
            ],
        )(x, q, kv, other, out_far)

    def gate(value):
        return pl.pallas_call(
            gate_kernel,
            in_specs=[pl.BlockSpec(memory_space=pl.ANY)],
            out_specs=SMEM,
            out_shape=jax.ShapeDtypeStruct((1,), jnp.int32),
            compiler_params=params(),
            cost_estimate=cost(1, 8),
            name="gate",
        )(value)

    def time_project(pieces):
        n = len(pieces)
        outs = [made(n, inner), made(n, 2 * inner)]
        return call(
            time_project_kernel,
            3 * n * work,
            in_specs=[full(piece) for piece in pieces]
            + [full(gains), pick(1, (feat, 3 * inner))],
            out_specs=[full(out) for out in outs],
            out_shape=outs,
        )(*pieces, gains, qkv_weights)

    def timed(groups, ks, *sources):
        outs = [made(1, inner)] * len(ks)
        return call(
            functools.partial(time_kernel, groups, ks),
            2 * len(ks) * work,
            in_specs=[full(source) for source in sources],
            out_specs=[full(out) for out in outs],
            out_shape=outs,
        )(*sources)

    def finish(items, pieces, mixes, extra):
        return call(
            functools.partial(finish_kernel, items, len(mixes), high),
            work * len(items),
            in_specs=[pick(1, (inner, feat))]
            + [whole(each, feat)] * len(items)
            + [whole(*mix.shape) for mix in mixes]
            + [pl.BlockSpec(memory_space=pl.ANY)] * len(extra),
            out_specs=HBM,
            out_shape=jax.ShapeDtypeStruct((rows, cols, feat), bf),
            scratch_shapes=[
                pltpu.VMEM((len(items), rows, COLB, feat), bf),
                pltpu.SemaphoreType.DMA((len(items),)),
            ],
            input_output_aliases={
                1 + len(items) + len(mixes): 0 for a in extra if a.ndim == 3
            },
        )(out_weights, *pieces, *mixes, *extra)

    def after(values, earlier):
        return lax.optimization_barrier((values, earlier))[0]

    def swap(a):
        return lax.ppermute(a, "space", [(0, 1), (1, 0)])

    def route(k):
        pairs = []
        for z in range(high):
            for lo in range(2):
                for s in range(2):
                    there = z ^ k
                    to = (there * 2 + (s ^ (there >= half))) * 2 + (lo ^ (z >= half))
                    pairs.append(((z * 2 + lo) * 2 + s, to))
        return pairs

    def permute(piece, k):
        return lax.ppermute(piece, ("tm", "space"), route(k))

    def exchange(pieces, ks):
        return {k: permute(pieces[k], k) for k in ks}

    kv, normed, keys, gain, tile = load(x)
    other = swap(kv)
    q, queries = ask(normed)
    pieces, arrived = [{}, {}], [{}, {}]
    outs = height(half, 0, tile, q, kv, other)
    pieces[0].update(zip(heavy, outs))
    arrived[0].update(exchange(pieces[0], heavy))
    q, kv, tile = project(0, light, after(x, outs[0]), gain, keys, queries)
    other = swap(kv)
    q1, kv1, tile1 = project(1, order, after(x, q), gain, keys, queries)
    other1 = swap(kv1)
    outs = height(half, 0, tile, after(q, q1), kv, other)
    pieces[0].update(zip(light, outs))
    arrived[0].update(exchange(pieces[0], light))
    for ks, at in ((heavy, 0), (light, half)):
        q1 = after(q1, outs[0])
        outs = height(half, at, tile1, q1, kv1, other1)
        pieces[1].update(zip(ks, outs))
        ready = dict(pieces[1])
        arrived[1].update(exchange(ready, ks))
    last = outs[0]
    groups = [[order], [[k for k in order if k != half], [half]]]
    home, gates = [], []
    for c in range(CHUNKS):
        sources = []
        for group in groups[c]:
            got = after([arrived[c][k] for k in group], last)
            q, kv = time_project(got)
            sources += [q, kv, swap(kv)]
            last = q
        mixes = timed(groups[c], order, *sources)
        last = mixes[0]
        home.append(exchange(dict(zip(order, mixes)), order))
        if c + 1 < CHUNKS:
            last = gate(last)
            gates.append(last)
    out = gates
    for c in range(CHUNKS):
        items = [(c, k) for k in order]
        held = after([pieces[c][k] for k in order], last)
        out = [finish(items, held, [home[c][k] for k in order], out)]
    return out[0][None]


def attend_plain(stream, gain, qkv_weight, out_weight):
    groups, length, _ = stream.shape
    inner = out_weight.shape[0]
    heads = inner // HEAD
    wide = stream.astype(jnp.float32)
    normed = normalise(wide, gain)
    projected = jnp.einsum(
        "glf,fe->gle", normed, qkv_weight, preferred_element_type=jnp.float32
    ).astype(jnp.bfloat16)
    q, k, v = jnp.split(projected.reshape(groups, length, 3 * heads, HEAD), 3, axis=2)
    scores = jnp.einsum("gqhd,gkhd->ghqk", q, k, preferred_element_type=jnp.float32) * HEAD**-0.5
    weights = jax.nn.softmax(scores, axis=-1).astype(jnp.bfloat16)
    mixture = jnp.einsum("ghqk,gkhd->gqhd", weights, v, preferred_element_type=jnp.float32)
    mixture = mixture.astype(jnp.bfloat16).reshape(groups, length, inner)
    update = jnp.einsum("gle,ef->glf", mixture, out_weight, preferred_element_type=jnp.float32)
    return (wide + update).astype(jnp.bfloat16)


def plain(tokens, gains, qkv_weights, out_weights):
    frames = lax.axis_size("tm")
    local = lax.all_to_all(tokens[0], "space", split_axis=1, concat_axis=0, tiled=True)
    height_n, wide, feat = local.shape
    by_column = jnp.transpose(local, (1, 0, 2))
    done = attend_plain(by_column, gains[0], qkv_weights[0], out_weights[0])
    flat = done.reshape(frames, wide * height_n // frames, feat)
    by_frame = lax.all_to_all(flat, "tm", split_axis=0, concat_axis=0, tiled=True)
    done = attend_plain(
        jnp.transpose(by_frame, (1, 0, 2)), gains[1], qkv_weights[1], out_weights[1]
    )
    back = lax.all_to_all(
        jnp.transpose(done, (1, 0, 2)), "tm", split_axis=0, concat_axis=0, tiled=True
    )
    by_row = jnp.transpose(back.reshape(wide, height_n, feat), (1, 0, 2))
    return lax.all_to_all(by_row, "space", split_axis=0, concat_axis=1, tiled=True)[None]


def solution(mesh):
    frames, pair = mesh.shape["tm"], mesh.shape["space"]
    high = frames // 2

    def shards(tokens, gains, qkv_weights, out_weights):
        _, rows, cols, feat = tokens.shape
        inner = out_weights.shape[1]
        count = rows * cols // CHUNKS
        fits = (
            pair == 2
            and frames == 2 * high
            and high > 1
            and high & (high - 1) == 0
            and cols == CHUNKS * COLB * high
            and count % (high * POSB) == 0
            and inner % (QUAD * HEAD) == 0
            and feat % 128 == 0
        )
        body = fast if fits else plain
        return body(tokens, gains, qkv_weights, out_weights)

    return jax.shard_map(
        shards,
        mesh=mesh,
        in_specs=(P(("grp", "tm"), "space", None, None), P(), P(), P()),
        out_specs=P(("grp", "tm"), "space", None, None),
        check_vma=False,
    )
```

```python
import functools

import jax
import jax.numpy as jnp
from jax import lax
from jax.experimental import pallas as pl
from jax.experimental.pallas import tpu as pltpu
from jax.sharding import PartitionSpec as P


HEAD = 64
EPS = 1e-06
QUAD = 4
CHUNKS = 2
COLB = 8
SPLIT = 2
POSB = 16
NEG = -1e30
VMEM_BYTES = 16 * 1024 * 1024


def params():
    return pltpu.CompilerParams(vmem_limit_bytes=VMEM_BYTES)


def normalise(stream, gain):
    scale = lax.rsqrt(jnp.mean(stream * stream, axis=-1, keepdims=True) + EPS)
    return (stream * scale * gain).astype(jnp.bfloat16)


def group_bias(keys, group):
    left = lax.broadcasted_iota(jnp.int32, (1, group, keys), 1)
    right = lax.broadcasted_iota(jnp.int32, (1, group, keys), 2) % group
    return jnp.where(left == right, 0.0, NEG)


def attend_quad(query, key, value, bias):
    rows, width = query.shape
    keys = key.shape[0]
    lanes = lax.broadcasted_iota(jnp.int32, (rows, width), 1) // HEAD
    heads = width // HEAD
    zero = jnp.zeros_like(query)
    stacked = jnp.concatenate([jnp.where(lanes == h, query, zero) for h in range(heads)], axis=0)
    scores = lax.dot_general(
        stacked, key, (((1,), (1,)), ((), ())), preferred_element_type=jnp.float32
    )
    scores = scores.reshape(heads * rows // bias.shape[1], bias.shape[1], keys) + bias
    raised = jnp.exp(scores - jnp.max(scores, axis=-1, keepdims=True))
    total = jnp.sum(raised, axis=-1, keepdims=True).reshape(heads * rows, 1)
    raised = raised.reshape(heads * rows, keys).astype(jnp.bfloat16)
    mixed = jnp.dot(raised, value, preferred_element_type=jnp.float32) * (1.0 / total)
    out = mixed[:rows]
    for h in range(1, heads):
        out = jnp.where(lanes == h, mixed[h * rows : (h + 1) * rows], out)
    return out.astype(jnp.bfloat16)


def join(parts):
    return parts[0] if len(parts) == 1 else jnp.concatenate(parts, axis=0)


def project_keys(normed, weight, kv_ref):
    kv_ref[...] = jnp.dot(normed, weight, preferred_element_type=jnp.float32).astype(jnp.bfloat16)


def project_queries(normed, weight, q_ref):
    q_ref[...] = jnp.dot(normed, weight, preferred_element_type=jnp.float32).astype(
        jnp.bfloat16
    ) * jnp.bfloat16(HEAD**-0.5)


def position():
    return lax.axis_index("tm") // 2


def token_loads(c, ks, high, x_ref, x_out, sem):
    colb = x_out.shape[2]
    loads = []
    for i, k in enumerate(ks):
        column = pl.multiple_of((c * high + jnp.bitwise_xor(position(), k)) * colb, colb)
        loads.append(
            pltpu.make_async_copy(x_ref.at[:, pl.ds(column, colb), :], x_out.at[i], sem.at[i])
        )
    return loads


def load_kernel(ks, high, x_ref, gain_ref, w_ref, kv_ref, normed_ref, w_out, gain_out, *refs):
    x_out, x_sem, w_sem, gain_sem = refs
    _, rows, colb, feat = x_out.shape
    width = kv_ref.shape[1]
    per = rows * colb
    loads = token_loads(0, ks, high, x_ref, x_out, x_sem)
    step = feat // SPLIT
    fetches = [
        pltpu.make_async_copy(
            w_ref.at[0, pl.ds(i * step, step), pl.ds(width // 2, width)],
            w_out.at[pl.ds(i * step, step), :],
            w_sem.at[i],
        )
        for i in range(SPLIT)
    ]
    gain_load = pltpu.make_async_copy(gain_ref, gain_out, gain_sem)
    for copy in [gain_load] + loads + fetches:
        copy.start()
    gain_load.wait()
    for i, load in enumerate(loads):
        load.wait()
        stream = x_out[i].astype(jnp.float32).reshape(per, feat)
        normed_ref[i * per : (i + 1) * per, :] = normalise(stream, gain_out[0:1, :])
    total = None
    for i, fetch in enumerate(fetches):
        fetch.wait()
        span = slice(i * step, (i + 1) * step)
        part = jnp.dot(normed_ref[:, span], w_out[span, :], preferred_element_type=jnp.float32)
        total = part if total is None else total + part
    kv_ref[...] = total.astype(jnp.bfloat16)


def ask_kernel(normed_ref, w_ref, q_ref, w_out, sem):
    fetch = pltpu.make_async_copy(w_ref.at[0, :, pl.ds(0, q_ref.shape[1])], w_out, sem)
    fetch.start()
    fetch.wait()
    project_queries(normed_ref[...], w_out[...], q_ref)


def project_kernel(c, ks, high, x_ref, gain_ref, keys_ref, queries_ref, q_ref, kv_ref, x_out, sem):
    count, rows, colb, feat = x_out.shape
    loads = token_loads(c, ks, high, x_ref, x_out, sem)
    for load in loads:
        load.start()
    for load in loads:
        load.wait()
    stream = x_out[...].astype(jnp.float32).reshape(count * rows * colb, feat)
    normed = normalise(stream, gain_ref[0:1, :])
    project_keys(normed, keys_ref[...], kv_ref)
    project_queries(normed, queries_ref[...], q_ref)


def height_kernel(tile, start, x_ref, q_ref, kv_ref, other_ref, w_ref, *refs):
    mix_ref, w_buf, w_sem = refs[-3:]
    _, rows, colb, feat = x_ref.shape
    per = rows * colb
    fetch = pltpu.make_async_copy(w_ref.at[0], w_buf, w_sem)
    fetch.start()
    inner = q_ref.shape[1]
    width = QUAD * HEAD
    bias = group_bias(2 * per, colb)
    zero = lax.axis_index("space") // lax.axis_size("space")
    for i in range(len(refs) - 3):
        span = pl.ds(pl.multiple_of((zero + i) * per, per) + start, per)
        for lo in range(0, inner, width):
            here, there = slice(lo, lo + width), slice(inner + lo, inner + lo + width)
            key = join([kv_ref[span, here], other_ref[span, here]])
            value = join([kv_ref[span, there], other_ref[span, there]])
            mix_ref[i * per : (i + 1) * per, here] = attend_quad(
                q_ref[span, here], key, value, bias
            )
    fetch.wait()
    update = jnp.dot(mix_ref[...], w_buf[...], preferred_element_type=jnp.float32)
    for i in range(len(refs) - 3):
        stream = x_ref[tile + i].astype(jnp.float32).reshape(per, feat)
        refs[i][...] = (stream + update[i * per : (i + 1) * per]).astype(jnp.bfloat16)


def time_project_kernel(*refs):
    gain_ref, w_ref, q_ref, kv_ref = refs[-4:]
    normed = join([normalise(ref[...].astype(jnp.float32), gain_ref[1:2, :]) for ref in refs[:-4]])
    inner = q_ref.shape[1]
    project_keys(normed, w_ref[:, inner:], kv_ref)
    project_queries(normed, w_ref[:, :inner], q_ref)


def gate_kernel(in_ref, out_ref):
    pass


def time_kernel(groups, ks, *refs):
    count = 3 * len(groups)
    sources, mix_refs = refs[:count], refs[count:]
    each, inner = mix_refs[0].shape
    width = QUAD * HEAD
    flat = [(g, i, k) for g, group in enumerate(groups) for i, k in enumerate(group)]

    bias = group_bias(2 * len(flat) * POSB, POSB)

    def rows(which, p, lo, chosen=flat):
        return [
            sources[3 * g + which][i * each + p : i * each + p + POSB, lo : lo + width]
            for g, i, _ in chosen
        ]

    for p in range(0, each, POSB):
        for lo in range(0, inner, width):
            key = join(rows(1, p, lo) + rows(2, p, lo))
            value = join(rows(1, p, inner + lo) + rows(2, p, inner + lo))
            asking = [entry for k in ks for entry in flat if entry[2] == k]
            out = attend_quad(join(rows(0, p, lo, asking)), key, value, bias)
            for n, ref in enumerate(mix_refs):
                ref[p : p + POSB, lo : lo + width] = out[n * POSB : (n + 1) * POSB]


def finish_kernel(items, mixed, high, w_ref, *refs):
    pieces, mixes = refs[: len(items)], refs[len(items) : len(items) + mixed]
    out_ref, buf, sem = refs[-3:]
    _, rows, colb, feat = buf.shape
    per = rows * colb
    update = jnp.dot(
        jnp.concatenate([ref[...] for ref in mixes], axis=0),
        w_ref[...],
        preferred_element_type=jnp.float32,
    )
    copies = []
    for i, (c, k) in enumerate(items):
        total = pieces[i][...].astype(jnp.float32) + update[i * per : (i + 1) * per]
        buf[i] = total.reshape(rows, colb, feat).astype(jnp.bfloat16)
        place = c * high + jnp.bitwise_xor(position(), k)
        column = pl.multiple_of(place * colb, colb)
        copies.append(
            pltpu.make_async_copy(buf.at[i], out_ref.at[:, pl.ds(column, colb), :], sem.at[i])
        )
        copies[-1].start()
    for copy in copies:
        copy.wait()


HBM = pl.BlockSpec(memory_space=pltpu.HBM)


def cost(flops, moved):
    return pl.CostEstimate(flops=int(flops), bytes_accessed=int(moved), transcendentals=0)


def fast(tokens, gains, qkv_weights, out_weights):
    high = lax.axis_size("tm") // 2
    half = high // 2
    order = list(range(high - 1, -1, -1))
    heavy, light = order[:half], order[half:]
    rows, cols, feat = tokens.shape[1:]
    inner = out_weights.shape[1]
    wide = cols // CHUNKS
    count = rows * wide
    each = count // high
    bf = jnp.bfloat16
    x = pltpu.with_memory_space_constraint(tokens[0], pltpu.HBM)
    gains_far = pltpu.with_memory_space_constraint(gains, pltpu.HBM)
    qkv_far = pltpu.with_memory_space_constraint(qkv_weights, pltpu.HBM)
    out_far = pltpu.with_memory_space_constraint(out_weights, pltpu.HBM)

    def pick(i, n):
        return pl.BlockSpec((None,) + n, lambda _: (i,) + (0,) * len(n))

    def whole(*shape):
        return pl.BlockSpec(shape, lambda _: (0,) * len(shape))

    def call(kernel, flops, **rest):
        return pl.pallas_call(
            kernel,
            grid=(1,),
            compiler_params=params(),
            cost_estimate=cost(flops, 4 * count * feat),
            **rest,
        )

    work = 2 * count * feat * inner // high

    def made(n, width):
        return jax.ShapeDtypeStruct((n * each, width), bf)

    def full(array):
        return whole(*array.shape)

    def tiles(n):
        return jax.ShapeDtypeStruct((n, rows, COLB, feat), bf)

    def load(x):
        outs = [
            made(half, 2 * inner),
            made(half, feat),
            jax.ShapeDtypeStruct((feat, 2 * inner), bf),
            jax.ShapeDtypeStruct(gains.shape, gains.dtype),
            tiles(half),
        ]
        return call(
            functools.partial(load_kernel, heavy, high),
            2 * half * work,
            in_specs=[HBM, HBM, HBM],
            out_specs=[full(out) for out in outs],
            out_shape=outs,
            scratch_shapes=[
                pltpu.SemaphoreType.DMA((half,)),
                pltpu.SemaphoreType.DMA((SPLIT,)),
                pltpu.SemaphoreType.DMA,
            ],
        )(x, gains_far, qkv_far)

    def ask(normed):
        outs = [made(half, inner), jax.ShapeDtypeStruct((feat, inner), bf)]
        return call(
            ask_kernel,
            half * work,
            in_specs=[full(normed), HBM],
            out_specs=[full(out) for out in outs],
            out_shape=outs,
            scratch_shapes=[pltpu.SemaphoreType.DMA],
        )(normed, qkv_far)

    def project(c, ks, x, gain, keys, queries):
        n = len(ks)
        outs = [made(n, inner), made(n, 2 * inner), tiles(n)]
        return call(
            functools.partial(project_kernel, c, ks, high),
            3 * n * work,
            in_specs=[HBM, full(gain), full(keys), full(queries)],
            out_specs=[full(out) for out in outs],
            out_shape=outs,
            scratch_shapes=[pltpu.SemaphoreType.DMA((n,))],
        )(x, gain, keys, queries)

    def height(n, at, x, q, kv, other):
        outs = [made(1, feat)] * n
        return call(
            functools.partial(height_kernel, at, at * each),
            2 * n * work,
            in_specs=[full(x), full(q), full(kv), full(other), HBM],
            out_specs=[full(out) for out in outs],
            out_shape=outs,
            scratch_shapes=[
                pltpu.VMEM((n * each, inner), bf),
                pltpu.VMEM((inner, feat), bf),
                pltpu.SemaphoreType.DMA,
            ],
        )(x, q, kv, other, out_far)

    def gate(value):
        return pl.pallas_call(
            gate_kernel,
            in_specs=[pl.BlockSpec(memory_space=pl.ANY)],
            out_specs=pl.BlockSpec(memory_space=pl.ANY),
            out_shape=jax.ShapeDtypeStruct((8, 128), jnp.float32),
            compiler_params=params(),
            cost_estimate=cost(1, 8),
            name="gate",
        )(value)

    def time_project(pieces):
        n = len(pieces)
        outs = [made(n, inner), made(n, 2 * inner)]
        return call(
            time_project_kernel,
            3 * n * work,
            in_specs=[full(piece) for piece in pieces]
            + [full(gains), pick(1, (feat, 3 * inner))],
            out_specs=[full(out) for out in outs],
            out_shape=outs,
        )(*pieces, gains, qkv_weights)

    def timed(groups, ks, *sources):
        outs = [made(1, inner)] * len(ks)
        return call(
            functools.partial(time_kernel, groups, ks),
            2 * len(ks) * work,
            in_specs=[full(source) for source in sources],
            out_specs=[full(out) for out in outs],
            out_shape=outs,
        )(*sources)

    def finish(items, pieces, mixes, extra):
        return call(
            functools.partial(finish_kernel, items, len(mixes), high),
            work * len(items),
            in_specs=[pick(1, (inner, feat))]
            + [whole(each, feat)] * len(items)
            + [whole(*mix.shape) for mix in mixes]
            + [pl.BlockSpec(memory_space=pl.ANY)] * len(extra),
            out_specs=HBM,
            out_shape=jax.ShapeDtypeStruct((rows, cols, feat), bf),
            scratch_shapes=[
                pltpu.VMEM((len(items), rows, COLB, feat), bf),
                pltpu.SemaphoreType.DMA((len(items),)),
            ],
            input_output_aliases={
                1 + len(items) + len(mixes): 0 for a in extra if a.ndim == 3
            },
        )(out_weights, *pieces, *mixes, *extra)

    def after(values, earlier):
        return lax.optimization_barrier((values, earlier))[0]

    def swap(a):
        return lax.ppermute(a, "space", [(0, 1), (1, 0)])

    def route(k):
        pairs = []
        for z in range(high):
            for lo in range(2):
                for s in range(2):
                    there = z ^ k
                    to = (there * 2 + (s ^ (there >= half))) * 2 + (lo ^ (z >= half))
                    pairs.append(((z * 2 + lo) * 2 + s, to))
        return pairs

    def permute(piece, k):
        return lax.ppermute(piece, ("tm", "space"), route(k))

    def exchange(pieces, ks):
        return {k: permute(pieces[k], k) for k in ks}

    kv, normed, keys, gain, tile = load(x)
    other = swap(kv)
    q, queries = ask(normed)
    pieces, arrived = [{}, {}], [{}, {}]
    outs = height(half, 0, tile, q, kv, other)
    pieces[0].update(zip(heavy, outs))
    arrived[0].update(exchange(pieces[0], heavy))
    q, kv, tile = project(0, light, after(x, outs[0]), gain, keys, queries)
    other = swap(kv)
    q1, kv1, tile1 = project(1, order, after(x, q), gain, keys, queries)
    other1 = swap(kv1)
    outs = height(half, 0, tile, after(q, q1), kv, other)
    pieces[0].update(zip(light, outs))
    arrived[0].update(exchange(pieces[0], light))
    for ks, at in ((heavy, 0), (light, half)):
        q1 = after(q1, outs[0])
        outs = height(half, at, tile1, q1, kv1, other1)
        pieces[1].update(zip(ks, outs))
        ready = dict(pieces[1])
        arrived[1].update(exchange(ready, ks))
    last = outs[0]
    groups = [[order], [[k for k in order if k != half], [half]]]
    home, gates = [], []
    for c in range(CHUNKS):
        sources = []
        for n, group in enumerate(groups[c]):
            got = after([arrived[c][k] for k in group], last)
            q, kv = time_project(got)
            sources += [q, kv, swap(kv)]
            last = q
            if c and not n:
                home[0].update(exchange(after({half: mixes[half]}, q), [half]))
        outs = timed(groups[c], order, *sources)
        last, mixes = outs[0], dict(zip(order, outs))
        home.append(exchange(mixes, [k for k in order if c or k != half]))
        if c + 1 < CHUNKS:
            last = gate(last)
            gates.append(last)
    out = gates
    for c in range(CHUNKS):
        items = [(c, k) for k in order]
        held = after([pieces[c][k] for k in order], last)
        out = [finish(items, held, [home[c][k] for k in order], out)]
    return out[0][None]


def attend_plain(stream, gain, qkv_weight, out_weight):
    groups, length, _ = stream.shape
    inner = out_weight.shape[0]
    heads = inner // HEAD
    wide = stream.astype(jnp.float32)
    normed = normalise(wide, gain)
    projected = jnp.einsum(
        "glf,fe->gle", normed, qkv_weight, preferred_element_type=jnp.float32
    ).astype(jnp.bfloat16)
    q, k, v = jnp.split(projected.reshape(groups, length, 3 * heads, HEAD), 3, axis=2)
    scores = jnp.einsum("gqhd,gkhd->ghqk", q, k, preferred_element_type=jnp.float32) * HEAD**-0.5
    weights = jax.nn.softmax(scores, axis=-1).astype(jnp.bfloat16)
    mixture = jnp.einsum("ghqk,gkhd->gqhd", weights, v, preferred_element_type=jnp.float32)
    mixture = mixture.astype(jnp.bfloat16).reshape(groups, length, inner)
    update = jnp.einsum("gle,ef->glf", mixture, out_weight, preferred_element_type=jnp.float32)
    return (wide + update).astype(jnp.bfloat16)


def plain(tokens, gains, qkv_weights, out_weights):
    frames = lax.axis_size("tm")
    local = lax.all_to_all(tokens[0], "space", split_axis=1, concat_axis=0, tiled=True)
    height_n, wide, feat = local.shape
    by_column = jnp.transpose(local, (1, 0, 2))
    done = attend_plain(by_column, gains[0], qkv_weights[0], out_weights[0])
    flat = done.reshape(frames, wide * height_n // frames, feat)
    by_frame = lax.all_to_all(flat, "tm", split_axis=0, concat_axis=0, tiled=True)
    done = attend_plain(
        jnp.transpose(by_frame, (1, 0, 2)), gains[1], qkv_weights[1], out_weights[1]
    )
    back = lax.all_to_all(
        jnp.transpose(done, (1, 0, 2)), "tm", split_axis=0, concat_axis=0, tiled=True
    )
    by_row = jnp.transpose(back.reshape(wide, height_n, feat), (1, 0, 2))
    return lax.all_to_all(by_row, "space", split_axis=0, concat_axis=1, tiled=True)[None]


def solution(mesh):
    frames, pair = mesh.shape["tm"], mesh.shape["space"]
    high = frames // 2

    def shards(tokens, gains, qkv_weights, out_weights):
        _, rows, cols, feat = tokens.shape
        inner = out_weights.shape[1]
        count = rows * cols // CHUNKS
        fits = (
            pair == 2
            and frames == 2 * high
            and high > 1
            and high & (high - 1) == 0
            and cols == CHUNKS * COLB * high
            and count % (high * POSB) == 0
            and inner % (QUAD * HEAD) == 0
            and feat % 128 == 0
        )
        body = fast if fits else plain
        return body(tokens, gains, qkv_weights, out_weights)

    return jax.shard_map(
        shards,
        mesh=mesh,
        in_specs=(P(("grp", "tm"), "space", None, None), P(), P(), P()),
        out_specs=P(("grp", "tm"), "space", None, None),
        check_vma=False,
    )
```

```python
import functools

import jax
import jax.numpy as jnp
from jax import lax
from jax.experimental import pallas as pl
from jax.experimental.pallas import tpu as pltpu
from jax.sharding import PartitionSpec as P


HEAD = 64
EPS = 1e-06
QUAD = 4
CHUNKS = 2
COLB = 8
SPLIT = 1
POSB = 16
NEG = -1e30
VMEM_BYTES = 16 * 1024 * 1024


def params():
    return pltpu.CompilerParams(vmem_limit_bytes=VMEM_BYTES)


def normalise(stream, gain):
    scale = lax.rsqrt(jnp.mean(stream * stream, axis=-1, keepdims=True) + EPS)
    return (stream * scale * gain).astype(jnp.bfloat16)


def group_bias(keys, group):
    left = lax.broadcasted_iota(jnp.int32, (1, group, keys), 1)
    right = lax.broadcasted_iota(jnp.int32, (1, group, keys), 2) % group
    return jnp.where(left == right, 0.0, NEG)


def attend_quad(query, key, value, bias, early):
    rows, width = query.shape
    keys = key.shape[0]
    lanes = lax.broadcasted_iota(jnp.int32, (rows, width), 1) // HEAD
    heads = width // HEAD
    zero = jnp.zeros_like(query)
    stacked = jnp.concatenate([jnp.where(lanes == h, query, zero) for h in range(heads)], axis=0)
    scores = lax.dot_general(
        stacked, key, (((1,), (1,)), ((), ())), preferred_element_type=jnp.float32
    )
    scores = scores.reshape(heads * rows // bias.shape[1], bias.shape[1], keys) + bias
    raised = jnp.exp(scores - jnp.max(scores, axis=-1, keepdims=True))
    share = 1.0 / jnp.sum(raised, axis=-1, keepdims=True)
    if early:
        raised = raised * share
    raised = raised.reshape(heads * rows, keys).astype(jnp.bfloat16)
    mixed = jnp.dot(raised, value, preferred_element_type=jnp.float32)
    if not early:
        mixed = mixed * share.reshape(heads * rows, 1)
    out = mixed[:rows]
    for h in range(1, heads):
        out = jnp.where(lanes == h, mixed[h * rows : (h + 1) * rows], out)
    return out.astype(jnp.bfloat16)


def join(parts):
    return parts[0] if len(parts) == 1 else jnp.concatenate(parts, axis=0)


def project_keys(normed, weight, kv_ref):
    kv_ref[...] = jnp.dot(normed, weight, preferred_element_type=jnp.float32).astype(jnp.bfloat16)


def project_queries(normed, weight, q_ref):
    q_ref[...] = jnp.dot(normed, weight, preferred_element_type=jnp.float32).astype(
        jnp.bfloat16
    ) * jnp.bfloat16(HEAD**-0.5)


def position():
    return lax.axis_index("tm") // 2


def token_loads(c, ks, high, x_ref, x_out, sem):
    colb = x_out.shape[2]
    loads = []
    for i, k in enumerate(ks):
        column = pl.multiple_of((c * high + jnp.bitwise_xor(position(), k)) * colb, colb)
        loads.append(
            pltpu.make_async_copy(x_ref.at[:, pl.ds(column, colb), :], x_out.at[i], sem.at[i])
        )
    return loads


def load_kernel(ks, high, x_ref, gain_ref, w_ref, kv_ref, normed_ref, w_out, gain_out, *refs):
    x_out, x_sem, w_sem, gain_sem = refs
    _, rows, colb, feat = x_out.shape
    width = kv_ref.shape[1]
    per = rows * colb
    loads = token_loads(0, ks, high, x_ref, x_out, x_sem)
    step = feat // SPLIT
    fetches = [
        pltpu.make_async_copy(
            w_ref.at[0, pl.ds(i * step, step), pl.ds(width // 2, width)],
            w_out.at[pl.ds(i * step, step), :],
            w_sem.at[i],
        )
        for i in range(SPLIT)
    ]
    gain_load = pltpu.make_async_copy(gain_ref, gain_out, gain_sem)
    for copy in [gain_load] + loads + fetches:
        copy.start()
    gain_load.wait()
    for i, load in enumerate(loads):
        load.wait()
        stream = x_out[i].astype(jnp.float32).reshape(per, feat)
        normed_ref[i * per : (i + 1) * per, :] = normalise(stream, gain_out[0:1, :])
    total = None
    for i, fetch in enumerate(fetches):
        fetch.wait()
        span = slice(i * step, (i + 1) * step)
        part = jnp.dot(normed_ref[:, span], w_out[span, :], preferred_element_type=jnp.float32)
        total = part if total is None else total + part
    kv_ref[...] = total.astype(jnp.bfloat16)


def ask_kernel(normed_ref, w_ref, q_ref, w_out, sem):
    fetch = pltpu.make_async_copy(w_ref.at[0, :, pl.ds(0, q_ref.shape[1])], w_out, sem)
    fetch.start()
    fetch.wait()
    project_queries(normed_ref[...], w_out[...], q_ref)


def project_kernel(c, ks, high, x_ref, gain_ref, keys_ref, queries_ref, q_ref, kv_ref, x_out, sem):
    count, rows, colb, feat = x_out.shape
    loads = token_loads(c, ks, high, x_ref, x_out, sem)
    for load in loads:
        load.start()
    for load in loads:
        load.wait()
    stream = x_out[...].astype(jnp.float32).reshape(count * rows * colb, feat)
    normed = normalise(stream, gain_ref[0:1, :])
    project_keys(normed, keys_ref[...], kv_ref)
    project_queries(normed, queries_ref[...], q_ref)


def height_kernel(tile, start, x_ref, q_ref, kv_ref, other_ref, w_ref, *refs):
    mix_ref, w_buf, w_sem = refs[-3:]
    _, rows, colb, feat = x_ref.shape
    per = rows * colb
    fetch = pltpu.make_async_copy(w_ref.at[0], w_buf, w_sem)
    fetch.start()
    inner = q_ref.shape[1]
    width = QUAD * HEAD
    bias = group_bias(2 * per, colb)
    zero = lax.axis_index("space") // lax.axis_size("space")
    for i in range(len(refs) - 3):
        span = pl.ds(pl.multiple_of((zero + i) * per, per) + start, per)
        for lo in range(0, inner, width):
            here, there = slice(lo, lo + width), slice(inner + lo, inner + lo + width)
            key = join([kv_ref[span, here], other_ref[span, here]])
            value = join([kv_ref[span, there], other_ref[span, there]])
            mix_ref[i * per : (i + 1) * per, here] = attend_quad(
                q_ref[span, here], key, value, bias, True
            )
    fetch.wait()
    update = jnp.dot(mix_ref[...], w_buf[...], preferred_element_type=jnp.float32)
    for i in range(len(refs) - 3):
        stream = x_ref[tile + i].astype(jnp.float32).reshape(per, feat)
        refs[i][...] = (stream + update[i * per : (i + 1) * per]).astype(jnp.bfloat16)


def time_project_kernel(*refs):
    gain_ref, w_ref, q_ref, kv_ref = refs[-4:]
    normed = join([normalise(ref[...].astype(jnp.float32), gain_ref[1:2, :]) for ref in refs[:-4]])
    inner = q_ref.shape[1]
    project_keys(normed, w_ref[:, inner:], kv_ref)
    project_queries(normed, w_ref[:, :inner], q_ref)


def gate_kernel(in_ref, out_ref):
    pass


def time_kernel(groups, ks, *refs):
    count = 3 * len(groups)
    sources, mix_refs = refs[:count], refs[count:]
    each, inner = mix_refs[0].shape
    width = QUAD * HEAD
    flat = [(g, i, k) for g, group in enumerate(groups) for i, k in enumerate(group)]

    bias = group_bias(2 * len(flat) * POSB, POSB)

    def rows(which, p, lo, chosen=flat):
        return [
            sources[3 * g + which][i * each + p : i * each + p + POSB, lo : lo + width]
            for g, i, _ in chosen
        ]

    for p in range(0, each, POSB):
        for lo in range(0, inner, width):
            key = join(rows(1, p, lo) + rows(2, p, lo))
            value = join(rows(1, p, inner + lo) + rows(2, p, inner + lo))
            asking = [entry for k in ks for entry in flat if entry[2] == k]
            out = attend_quad(join(rows(0, p, lo, asking)), key, value, bias, False)
            for n, ref in enumerate(mix_refs):
                ref[p : p + POSB, lo : lo + width] = out[n * POSB : (n + 1) * POSB]


def finish_kernel(items, mixed, high, w_ref, *refs):
    pieces, mixes = refs[: len(items)], refs[len(items) : len(items) + mixed]
    out_ref, buf, sem = refs[-3:]
    _, rows, colb, feat = buf.shape
    per = rows * colb
    update = jnp.dot(
        jnp.concatenate([ref[...] for ref in mixes], axis=0),
        w_ref[...],
        preferred_element_type=jnp.float32,
    )
    copies = []
    for i, (c, k) in enumerate(items):
        total = pieces[i][...].astype(jnp.float32) + update[i * per : (i + 1) * per]
        buf[i] = total.reshape(rows, colb, feat).astype(jnp.bfloat16)
        place = c * high + jnp.bitwise_xor(position(), k)
        column = pl.multiple_of(place * colb, colb)
        copies.append(
            pltpu.make_async_copy(buf.at[i], out_ref.at[:, pl.ds(column, colb), :], sem.at[i])
        )
        copies[-1].start()
    for copy in copies:
        copy.wait()


HBM = pl.BlockSpec(memory_space=pltpu.HBM)


def cost(flops, moved):
    return pl.CostEstimate(flops=int(flops), bytes_accessed=int(moved), transcendentals=0)


def fast(tokens, gains, qkv_weights, out_weights):
    high = lax.axis_size("tm") // 2
    half = high // 2
    order = list(range(high - 1, -1, -1))
    heavy, light = order[:half], order[half:]
    rows, cols, feat = tokens.shape[1:]
    inner = out_weights.shape[1]
    wide = cols // CHUNKS
    count = rows * wide
    each = count // high
    bf = jnp.bfloat16
    x = pltpu.with_memory_space_constraint(tokens[0], pltpu.HBM)
    gains_far = pltpu.with_memory_space_constraint(gains, pltpu.HBM)
    qkv_far = pltpu.with_memory_space_constraint(qkv_weights, pltpu.HBM)
    out_far = pltpu.with_memory_space_constraint(out_weights, pltpu.HBM)

    def pick(i, n):
        return pl.BlockSpec((None,) + n, lambda _: (i,) + (0,) * len(n))

    def whole(*shape):
        return pl.BlockSpec(shape, lambda _: (0,) * len(shape))

    def call(kernel, flops, **rest):
        return pl.pallas_call(
            kernel,
            grid=(1,),
            compiler_params=params(),
            cost_estimate=cost(flops, 4 * count * feat),
            **rest,
        )

    work = 2 * count * feat * inner // high

    def made(n, width):
        return jax.ShapeDtypeStruct((n * each, width), bf)

    def full(array):
        return whole(*array.shape)

    def tiles(n):
        return jax.ShapeDtypeStruct((n, rows, COLB, feat), bf)

    def load(x):
        outs = [
            made(half, 2 * inner),
            made(half, feat),
            jax.ShapeDtypeStruct((feat, 2 * inner), bf),
            jax.ShapeDtypeStruct(gains.shape, gains.dtype),
            tiles(half),
        ]
        return call(
            functools.partial(load_kernel, heavy, high),
            2 * half * work,
            in_specs=[HBM, HBM, HBM],
            out_specs=[full(out) for out in outs],
            out_shape=outs,
            scratch_shapes=[
                pltpu.SemaphoreType.DMA((half,)),
                pltpu.SemaphoreType.DMA((SPLIT,)),
                pltpu.SemaphoreType.DMA,
            ],
        )(x, gains_far, qkv_far)

    def ask(normed):
        outs = [made(half, inner), jax.ShapeDtypeStruct((feat, inner), bf)]
        return call(
            ask_kernel,
            half * work,
            in_specs=[full(normed), HBM],
            out_specs=[full(out) for out in outs],
            out_shape=outs,
            scratch_shapes=[pltpu.SemaphoreType.DMA],
        )(normed, qkv_far)

    def project(c, ks, x, gain, keys, queries):
        n = len(ks)
        outs = [made(n, inner), made(n, 2 * inner), tiles(n)]
        return call(
            functools.partial(project_kernel, c, ks, high),
            3 * n * work,
            in_specs=[HBM, full(gain), full(keys), full(queries)],
            out_specs=[full(out) for out in outs],
            out_shape=outs,
            scratch_shapes=[pltpu.SemaphoreType.DMA((n,))],
        )(x, gain, keys, queries)

    def height(n, at, x, q, kv, other):
        outs = [made(1, feat)] * n
        return call(
            functools.partial(height_kernel, at, at * each),
            2 * n * work,
            in_specs=[full(x), full(q), full(kv), full(other), HBM],
            out_specs=[full(out) for out in outs],
            out_shape=outs,
            scratch_shapes=[
                pltpu.VMEM((n * each, inner), bf),
                pltpu.VMEM((inner, feat), bf),
                pltpu.SemaphoreType.DMA,
            ],
        )(x, q, kv, other, out_far)

    def gate(value):
        return pl.pallas_call(
            gate_kernel,
            in_specs=[pl.BlockSpec(memory_space=pl.ANY)],
            out_specs=pl.BlockSpec(memory_space=pl.ANY),
            out_shape=jax.ShapeDtypeStruct((8, 128), jnp.float32),
            compiler_params=params(),
            cost_estimate=cost(1, 8),
            name="gate",
        )(value)

    def time_project(pieces):
        n = len(pieces)
        outs = [made(n, inner), made(n, 2 * inner)]
        return call(
            time_project_kernel,
            3 * n * work,
            in_specs=[full(piece) for piece in pieces]
            + [full(gains), pick(1, (feat, 3 * inner))],
            out_specs=[full(out) for out in outs],
            out_shape=outs,
        )(*pieces, gains, qkv_weights)

    def timed(groups, ks, *sources):
        outs = [made(1, inner)] * len(ks)
        return call(
            functools.partial(time_kernel, groups, ks),
            2 * len(ks) * work,
            in_specs=[full(source) for source in sources],
            out_specs=[full(out) for out in outs],
            out_shape=outs,
        )(*sources)

    def finish(items, pieces, mixes, extra):
        return call(
            functools.partial(finish_kernel, items, len(mixes), high),
            work * len(items),
            in_specs=[pick(1, (inner, feat))]
            + [whole(each, feat)] * len(items)
            + [whole(*mix.shape) for mix in mixes]
            + [pl.BlockSpec(memory_space=pl.ANY)] * len(extra),
            out_specs=HBM,
            out_shape=jax.ShapeDtypeStruct((rows, cols, feat), bf),
            scratch_shapes=[
                pltpu.VMEM((len(items), rows, COLB, feat), bf),
                pltpu.SemaphoreType.DMA((len(items),)),
            ],
            input_output_aliases={
                1 + len(items) + len(mixes): 0 for a in extra if a.ndim == 3
            },
        )(out_weights, *pieces, *mixes, *extra)

    def after(values, earlier):
        return lax.optimization_barrier((values, earlier))[0]

    def swap(a):
        return lax.ppermute(a, "space", [(0, 1), (1, 0)])

    def route(k):
        pairs = []
        for z in range(high):
            for lo in range(2):
                for s in range(2):
                    there = z ^ k
                    to = (there * 2 + (s ^ (there >= half))) * 2 + (lo ^ (z >= half))
                    pairs.append(((z * 2 + lo) * 2 + s, to))
        return pairs

    def permute(piece, k):
        return lax.ppermute(piece, ("tm", "space"), route(k))

    def exchange(pieces, ks):
        return {k: permute(pieces[k], k) for k in ks}

    kv, normed, keys, gain, tile = load(x)
    other = swap(kv)
    q, queries = ask(normed)
    pieces, arrived = [{}, {}], [{}, {}]
    outs = height(half, 0, tile, q, kv, other)
    pieces[0].update(zip(heavy, outs))
    arrived[0].update(exchange(pieces[0], heavy))
    q, kv, tile = project(0, light, after(x, outs[0]), gain, keys, queries)
    other = swap(kv)
    q1, kv1, tile1 = project(1, order, after(x, q), gain, keys, queries)
    other1 = swap(kv1)
    outs = height(half, 0, tile, after(q, q1), kv, other)
    pieces[0].update(zip(light, outs))
    arrived[0].update(exchange(pieces[0], light))
    for ks, at in ((heavy, 0), (light, half)):
        q1 = after(q1, outs[0])
        outs = height(half, at, tile1, q1, kv1, other1)
        pieces[1].update(zip(ks, outs))
        ready = dict(pieces[1])
        arrived[1].update(exchange(ready, ks))
    last = outs[0]
    groups = [[order], [[k for k in order if k != half], [half]]]
    home, gates = [], []
    for c in range(CHUNKS):
        sources = []
        for n, group in enumerate(groups[c]):
            got = after([arrived[c][k] for k in group], last)
            q, kv = time_project(got)
            sources += [q, kv, swap(kv)]
            last = q
            if c and not n:
                home[0].update(exchange(after({half: mixes[half]}, q), [half]))
        outs = timed(groups[c], order, *sources)
        last, mixes = outs[0], dict(zip(order, outs))
        home.append(exchange(mixes, [k for k in order if c or k != half]))
        if c + 1 < CHUNKS:
            last = gate(last)
            gates.append(last)
    out = gates
    for c in range(CHUNKS):
        items = [(c, k) for k in order]
        held = after([pieces[c][k] for k in order], last)
        out = [finish(items, held, [home[c][k] for k in order], out)]
    return out[0][None]


def attend_plain(stream, gain, qkv_weight, out_weight):
    groups, length, _ = stream.shape
    inner = out_weight.shape[0]
    heads = inner // HEAD
    wide = stream.astype(jnp.float32)
    normed = normalise(wide, gain)
    projected = jnp.einsum(
        "glf,fe->gle", normed, qkv_weight, preferred_element_type=jnp.float32
    ).astype(jnp.bfloat16)
    q, k, v = jnp.split(projected.reshape(groups, length, 3 * heads, HEAD), 3, axis=2)
    scores = jnp.einsum("gqhd,gkhd->ghqk", q, k, preferred_element_type=jnp.float32) * HEAD**-0.5
    weights = jax.nn.softmax(scores, axis=-1).astype(jnp.bfloat16)
    mixture = jnp.einsum("ghqk,gkhd->gqhd", weights, v, preferred_element_type=jnp.float32)
    mixture = mixture.astype(jnp.bfloat16).reshape(groups, length, inner)
    update = jnp.einsum("gle,ef->glf", mixture, out_weight, preferred_element_type=jnp.float32)
    return (wide + update).astype(jnp.bfloat16)


def plain(tokens, gains, qkv_weights, out_weights):
    frames = lax.axis_size("tm")
    local = lax.all_to_all(tokens[0], "space", split_axis=1, concat_axis=0, tiled=True)
    height_n, wide, feat = local.shape
    by_column = jnp.transpose(local, (1, 0, 2))
    done = attend_plain(by_column, gains[0], qkv_weights[0], out_weights[0])
    flat = done.reshape(frames, wide * height_n // frames, feat)
    by_frame = lax.all_to_all(flat, "tm", split_axis=0, concat_axis=0, tiled=True)
    done = attend_plain(
        jnp.transpose(by_frame, (1, 0, 2)), gains[1], qkv_weights[1], out_weights[1]
    )
    back = lax.all_to_all(
        jnp.transpose(done, (1, 0, 2)), "tm", split_axis=0, concat_axis=0, tiled=True
    )
    by_row = jnp.transpose(back.reshape(wide, height_n, feat), (1, 0, 2))
    return lax.all_to_all(by_row, "space", split_axis=0, concat_axis=1, tiled=True)[None]


def solution(mesh):
    frames, pair = mesh.shape["tm"], mesh.shape["space"]
    high = frames // 2

    def shards(tokens, gains, qkv_weights, out_weights):
        _, rows, cols, feat = tokens.shape
        inner = out_weights.shape[1]
        count = rows * cols // CHUNKS
        fits = (
            pair == 2
            and frames == 2 * high
            and high > 1
            and high & (high - 1) == 0
            and cols == CHUNKS * COLB * high
            and count % (high * POSB) == 0
            and inner % (QUAD * HEAD) == 0
            and feat % 128 == 0
        )
        body = fast if fits else plain
        return body(tokens, gains, qkv_weights, out_weights)

    return jax.shard_map(
        shards,
        mesh=mesh,
        in_specs=(P(("grp", "tm"), "space", None, None), P(), P(), P()),
        out_specs=P(("grp", "tm"), "space", None, None),
        check_vma=False,
    )
```
